32 devices in a mesh: rep: 8 (over y, x, core), fsdp: 4 (over z).
Axes of the slice: x: 2, y: 2, z: 4, core: 2. Of those that a mesh axis runs over, the one named last changes fastest.
Arguments:
- tokens: bfloat16 [8, 1024, 1024], P('rep', 'fsdp'), may hold values from -12 to 12
- cotangent: bfloat16 [8, 1024, 1024], P('rep', 'fsdp'), may hold values from -6 to 6
- qkv_weight: bfloat16 [1024, 3072], P('fsdp'), may hold values from -4 to 4
- out_weight: bfloat16 [1024, 1024], P('fsdp'), may hold values from -0.375 to 0.375
- up_weight: bfloat16 [1024, 4096], P('fsdp'), may hold values from -0.1875 to 0.1875
- down_weight: bfloat16 [1024, 4096], P('fsdp'), may hold values from -0.09375 to 0.09375
- ln_gain: bfloat16 [1024], P('fsdp'), may hold values from 0.5 to 1.5
- ln_bias: bfloat16 [1024], P('fsdp'), may hold values from -1.25 to 1.25
- up_bias: bfloat16 [4096], P('fsdp'), may hold values from -3 to 3
- down_bias: bfloat16 [1024], P('fsdp'), may hold values from -1.75 to 1.75
- qkv_moment: float32 [1024, 3072], P('fsdp'), may hold values from -24 to 24
- out_moment: float32 [1024, 1024], P('fsdp'), may hold values from -24 to 24
- up_moment: float32 [1024, 4096], P('fsdp'), may hold values from -24 to 24
- down_moment: float32 [1024, 4096], P('fsdp'), may hold values from -24 to 24
- gain_moment: float32 [1024], P('fsdp'), may hold values from -24 to 24
- beta_moment: float32 [1024], P('fsdp'), may hold values from -24 to 24
- up_bias_moment: float32 [4096], P('fsdp'), may hold values from -24 to 24
- down_bias_moment: float32 [1024], P('fsdp'), may hold values from -24 to 24
Outputs:
- block_out: bfloat16 [8, 1024, 1024], P('rep', 'fsdp')
- input_grad: float32 [8, 1024, 1024], P('rep', 'fsdp')
- qkv_grad: float32 [1024, 3072], P('fsdp')
- out_grad: float32 [1024, 1024], P('fsdp')
- up_grad: float32 [1024, 4096], P('fsdp')
- down_grad: float32 [1024, 4096], P('fsdp')
- gain_grad: float32 [1024], P('fsdp')
- beta_grad: float32 [1024], P('fsdp')
- up_bias_grad: float32 [4096], P('fsdp')
- down_bias_grad: float32 [1024], P('fsdp')
- qkv_new: float32 [1024, 3072], P('fsdp')
- out_new: float32 [1024, 1024], P('fsdp')
- up_new: float32 [1024, 4096], P('fsdp')
- down_new: float32 [1024, 4096], P('fsdp')
- gain_new: float32 [1024], P('fsdp')
- beta_new: float32 [1024], P('fsdp')
- up_bias_new: float32 [4096], P('fsdp')
- down_bias_new: float32 [1024], P('fsdp')
- qkv_moment_new: float32 [1024, 3072], P('fsdp')
- out_moment_new: float32 [1024, 1024], P('fsdp')
- up_moment_new: float32 [1024, 4096], P('fsdp')
- down_moment_new: float32 [1024, 4096], P('fsdp')
- gain_moment_new: float32 [1024], P('fsdp')
- beta_moment_new: float32 [1024], P('fsdp')
- up_bias_moment_new: float32 [4096], P('fsdp')
- down_bias_moment_new: float32 [1024], P('fsdp')
The draws below stay inside these ranges and needn't reach their ends.
All inputs are finite; a program needn't handle non-finite values.
Results may differ from the reference program's by a relative error of at most 0.011.
Values may be sent and summed in bfloat16 or wider, within the bound.
No kernel may reach another device: no remote copies, remote signals or barrier semaphores. Data moves between devices by JAX's collectives and lax.ppermute only.
A program may use at most 320 MiB of HBM per device.

```python
import math
import jax
import jax.numpy as jnp
from jax import lax

D = 1024
HEADS = 16
HEAD_DIM = 64
ROT = 32
FF = 4096
SEQ = 1024
NS = 5
SEQS = 8


def draw_tokens(key, part):
    key_base, key_row = jax.random.split(key, 2)
    shape_all = (SEQS, SEQ, D)
    row_scale = jnp.exp(jax.random.uniform(key_row, (SEQS, SEQ, 1), jnp.float32, jnp.log(0.3), jnp.log(3.0)))
    base_vals = jax.random.truncated_normal(key_base, -4.0, 4.0, shape_all, jnp.float32)
    return (base_vals * row_scale).astype(jnp.bfloat16)


def draw_qkv_weight(key, part):
    key_base = jax.random.fold_in(key, 0)
    return (jax.random.truncated_normal(key_base, -4.0, 4.0, (D, 3 * D), jnp.float32) * D ** (-0.5)).astype(jnp.bfloat16)


def spiked(entries, rng, source, target, blocks, factor):
    def block_of(dim):
        return (jnp.arange(entries.shape[dim]) // (entries.shape[dim] // blocks)).reshape((-1,) + (1,) * (entries.ndim - 1 - dim))

    first = jax.random.permutation(rng, blocks)[block_of(target)]
    second = (block_of(target) + blocks // 2) % blocks
    return jnp.where((block_of(source) == first) | (block_of(source) == second), factor * entries, entries)


def level_of(stream_key, dims, pieces, low, largest):
    loudness = 1.0
    for dim, blocks in pieces:
        draws = jax.random.uniform(jax.random.fold_in(jax.random.fold_in(stream_key, 6), dim), (blocks,), jnp.float32, low / len(pieces), largest / len(pieces))
        loudness = loudness * jnp.repeat(jnp.exp(draws), dims[dim] // blocks).reshape((-1,) + (1,) * (len(dims) - 1 - dim))
    return loudness


def centred(stream_key, dims, width, most, shards=(), held_as=jnp.bfloat16):
    factor_of = level_of(stream_key, dims, shards, -0.22, 0.18) if shards else 1.0
    entries = jax.random.normal(stream_key, dims, jnp.float32) * width * factor_of
    return jnp.minimum(jnp.maximum(entries, -most), most).astype(held_as)


def bell_draw_with(rng, dims, width, bound, pieces, heavy, held_as=jnp.bfloat16):
    drawn = width * jax.random.normal(rng, dims, jnp.float32)
    if pieces:
        drawn = drawn * level_of(rng, dims, pieces, -0.22, 0.18)
    return jnp.clip(spiked(drawn, jax.random.fold_in(rng, 3), *heavy), -bound, bound).astype(held_as)


def setup_inputs(seed: int = 0) -> dict:
    seeds = jax.random.split(jax.random.key(seed), 19)
    return {
        "tokens": draw_tokens(jax.random.fold_in(seeds[18], 71), 0),
        "cotangent": bell_draw_with(seeds[1], (SEQS, SEQ, D), 1.0, 6.0, ((0, 8), (1, 4)), (1, 2, 4, 2.0)),
        "qkv_weight": draw_qkv_weight(jax.random.fold_in(seeds[18], 71), 0),
        "out_weight": centred(seeds[3], (D, D), (D // 4) ** -0.5, 0.375, ((0, 4),)),
        "up_weight": centred(seeds[4], (D, FF), D ** -0.5, 0.1875, ((0, 4),)),
        "down_weight": centred(seeds[5], (D, FF), FF ** -0.5, 0.09375, ((0, 4),)),
        "ln_gain": jnp.clip(1.0 + 0.1 * jax.random.normal(seeds[6], (D,), jnp.float32), 0.5, 1.5).astype(jnp.bfloat16),
        "ln_bias": centred(seeds[7], (D,), 0.2, 1.25, ((0, 4),)),
        "up_bias": centred(seeds[8], (FF,), 0.5, 3.0, ((0, 4),)),
        "down_bias": centred(seeds[9], (D,), 0.3, 1.75, ((0, 4),)),
        "qkv_moment": centred(seeds[10], (D, 3 * D), 4.0, 24.0, ((0, 4),), jnp.float32),
        "out_moment": centred(seeds[11], (D, D), 4.0, 24.0, ((0, 4),), jnp.float32),
        "up_moment": centred(seeds[12], (D, FF), 4.0, 24.0, ((0, 4),), jnp.float32),
        "down_moment": centred(seeds[13], (D, FF), 4.0, 24.0, ((0, 4),), jnp.float32),
        "gain_moment": centred(seeds[14], (D,), 4.0, 24.0, ((0, 4),), jnp.float32),
        "beta_moment": centred(seeds[15], (D,), 4.0, 24.0, ((0, 4),), jnp.float32),
        "up_bias_moment": centred(seeds[16], (FF,), 4.0, 24.0, ((0, 4),), jnp.float32),
        "down_bias_moment": centred(seeds[17], (D,), 4.0, 24.0, ((0, 4),), jnp.float32),
    }


@jax.custom_vjp
def low(v):
    return lax.optimization_barrier(v.astype(jnp.bfloat16)).astype(jnp.float32)

@jax.custom_vjp
def low_back(v):
    return v

def low_keep(v):
    return (low(v), None)

def low_pass(kept, grad):
    return (grad,)

def back_keep(v):
    return (v, None)

def back_low(kept, grad):
    return (low(grad),)
low.defvjp(low_keep, low_pass)
low_back.defvjp(back_keep, back_low)
MOMENTUM_RATE = 0.9
MATRIX_RATE = 0.05
VECTOR_RATE = 0.002
COEF_A = 3.4445
COEF_B = -4.775
COEF_C = 2.0315

def matmul(left, right):
    return jnp.dot(left, right, precision=lax.Precision.HIGHEST, preferred_element_type=jnp.float32)

def layer_norm(values, gain_vec, beta_vec):
    center = values - lax.optimization_barrier(jnp.mean(values, axis=-1, keepdims=True))
    spread = lax.optimization_barrier(jnp.mean(center * center, axis=-1, keepdims=True))
    return center * lax.rsqrt(spread + 1e-05) * gain_vec + beta_vec

def rotary_tables(positions):
    half_rot = ROT // 2
    inverse = 10000.0 ** (-(2.0 * jnp.arange(half_rot, dtype=jnp.float32)) / ROT)
    angles = positions.astype(jnp.float32)[:, None] * inverse[None, :]
    return (jnp.cos(angles), jnp.sin(angles))

def rotate(heads_in, cosine, sine_table):
    half_rot = ROT // 2
    first_half = heads_in[..., :half_rot]
    second = heads_in[..., half_rot:ROT]
    return jnp.concatenate([first_half * cosine - second * sine_table, second * cosine + first_half * sine_table, heads_in[..., ROT:]], axis=-1)

def block(inputs, qkv_mat, out_mat, up_mat, down_mat, gain_vec, beta_vec, up_vec, down_vec):
    model_width = inputs.shape[1]
    normed = low(layer_norm(inputs, gain_vec, beta_vec))
    projected = low_back(matmul(normed, qkv_mat))
    cosine, sine_table = rotary_tables(jnp.arange(SEQ, dtype=jnp.int32))
    cosine = cosine[:, None, :]
    sine_table = sine_table[:, None, :]
    queries = low(rotate(projected[:, :model_width].reshape(SEQ, HEADS, HEAD_DIM), cosine, sine_table))
    keys = low(rotate(projected[:, model_width:2 * model_width].reshape(SEQ, HEADS, HEAD_DIM), cosine, sine_table))
    values = low(projected[:, 2 * model_width:].reshape(SEQ, HEADS, HEAD_DIM))
    scores = jnp.einsum('qhd,khd->hqk', queries, keys, precision=lax.Precision.HIGHEST) * HEAD_DIM ** (-0.5)
    scores = low_back(scores)
    causal = jnp.arange(SEQ)[:, None] >= jnp.arange(SEQ)[None, :]
    scores = jnp.where(causal[None], scores, -1e+30)
    attention = jax.nn.softmax(scores, axis=-1)
    mixed = jnp.einsum('hqk,khd->qhd', low(attention), values, precision=lax.Precision.HIGHEST).reshape(SEQ, model_width)
    mixed = low(low_back(mixed))
    hidden_pre = low_back(matmul(normed, up_mat) + up_vec)
    hidden = low(jax.nn.gelu(hidden_pre, approximate=True))
    return inputs + matmul(mixed, out_mat) + matmul(hidden, down_mat.T) + down_vec

def orthogonalize(moment):
    moment_f = lax.optimization_barrier(moment.astype(jnp.bfloat16)).astype(jnp.float32)
    frobenius = jnp.sqrt(jnp.sum(moment_f * moment_f))
    current = (moment_f / (frobenius + 1e-07)).astype(jnp.bfloat16)
    for repeat in range(NS):
        current_f = current.astype(jnp.float32)
        gram_low = matmul(current_f, current_f.T).astype(jnp.bfloat16)
        gram_f = gram_low.astype(jnp.float32)
        poly_low = (COEF_B * gram_f + COEF_C * matmul(gram_f, gram_f)).astype(jnp.bfloat16)
        current = (COEF_A * current_f + matmul(poly_low.astype(jnp.float32), current_f)).astype(jnp.bfloat16)
    return current

def reference(tokens, cotangent, qkv_weight, out_weight, up_weight, down_weight, ln_gain, ln_bias, up_bias, down_bias, qkv_moment, out_moment, up_moment, down_moment, gain_moment, beta_moment, up_bias_moment, down_bias_moment):
    params = (qkv_weight.astype(jnp.float32), out_weight.astype(jnp.float32), up_weight.astype(jnp.float32), down_weight.astype(jnp.float32), ln_gain.astype(jnp.float32), ln_bias.astype(jnp.float32), up_bias.astype(jnp.float32), down_bias.astype(jnp.float32))

    def one_sequence(totals, pair_in):
        inputs, upstream = pair_in
        result, pull_back = jax.vjp(block, inputs.astype(jnp.float32), *params)
        grads_all = pull_back(upstream.astype(jnp.float32))
        totals = tuple((running + fresh for running, fresh in zip(totals, grads_all[1:])))
        return (totals, (result.astype(jnp.bfloat16), grads_all[0]))
    zero_init = tuple((jnp.zeros(param.shape, jnp.float32) for param in params))
    grad_sum, outputs = lax.scan(one_sequence, zero_init, (tokens, cotangent))
    block_out, input_grad = outputs
    moments = (qkv_moment, out_moment, up_moment, down_moment, gain_moment, beta_moment, up_bias_moment, down_bias_moment)
    new_moments = tuple((MOMENTUM_RATE * moment + fresh for moment, fresh in zip(moments, grad_sum)))
    new_params = []
    for position in range(4):
        matrix = params[position]
        columns = matrix.shape[1]
        ortho_low = orthogonalize(new_moments[position]).astype(jnp.float32)
        new_params.append(matrix - MATRIX_RATE * 0.2 * math.sqrt(columns) * ortho_low)
    for position in range(4, 8):
        new_params.append(params[position] - VECTOR_RATE * new_moments[position])
    return (block_out, input_grad, grad_sum[0], grad_sum[1], grad_sum[2], grad_sum[3], grad_sum[4], grad_sum[5], grad_sum[6], grad_sum[7], new_params[0], new_params[1], new_params[2], new_params[3], new_params[4], new_params[5], new_params[6], new_params[7], new_moments[0], new_moments[1], new_moments[2], new_moments[3], new_moments[4], new_moments[5], new_moments[6], new_moments[7])
```

```python
import math

import jax
import jax.numpy as jnp
from jax import lax
from jax.experimental import pallas as pl
from jax.experimental.pallas import tpu as pltpu
from jax.sharding import PartitionSpec as P

HEAD_DIM = 64
ROT = 32
NS = 5
QB = 256

MOMENTUM_RATE = 0.9
MATRIX_RATE = 0.05
VECTOR_RATE = 0.002
COEF_A = 3.4445
COEF_B = -4.775
COEF_C = 2.0315

BF = jnp.bfloat16
F32 = jnp.float32


def contract(left, right, left_dim, right_dim):
    return lax.dot_general(
        left, right, (((left_dim,), (right_dim,)), ((), ())), preferred_element_type=F32
    )


def z_gather(x, nf):
    f = lax.axis_index("fsdp")
    length = x.shape[0]
    from_left, from_right = [], []
    right = left = x
    for step in range(1, nf):
        right = lax.ppermute(right, "fsdp", [(i, i + 1) for i in range(step - 1, nf - 1)])
        left = lax.ppermute(left, "fsdp", [(i, i - 1) for i in range(1, nf - step + 1)])
        from_left.append(right)
        from_right.append(left)
    line = jnp.concatenate(from_left[::-1] + [x] + from_right, axis=0)
    return lax.dynamic_slice_in_dim(line, (nf - 1 - f) * length, nf * length, 0)


def z_scatter_sum(x, nf):
    f = lax.axis_index("fsdp")

    def block(index):
        return lax.dynamic_index_in_dim(x, jnp.clip(index, 0, nf - 1), 0, keepdims=False)

    right = left = None
    for step in range(1, nf):
        send = block(f + nf - step)
        send = send if right is None else send + right.astype(F32)
        right = lax.ppermute(send.astype(BF), "fsdp", [(i, i + 1) for i in range(0, step)])
        send = block(f - nf + step)
        send = send if left is None else send + left.astype(F32)
        left = lax.ppermute(send.astype(BF), "fsdp", [(i, i - 1) for i in range(nf - step, nf)])
    return block(f) + right.astype(F32) + left.astype(F32)


def z_exchange(x):
    return lax.all_to_all(x, "fsdp", split_axis=0, concat_axis=0, tiled=True)


def xor_swap(x, bit, nr):
    return lax.ppermute(x, "rep", [(i, i ^ (1 << bit)) for i in range(nr)])


def rep_bit(bit):
    return (lax.axis_index("rep") >> bit) & 1


def bit_count(nr):
    return nr.bit_length() - 1


def plane_orders(nr):
    high = list(range(1, bit_count(nr)))
    return high, high[::-1]


def plane_gather(x, nr):
    half = x.shape[0] // 2
    first, second = plane_orders(nr)

    def gather(part, order):
        held = []
        for bit in order:
            other = xor_swap(part, bit, nr)
            axis = sum(1 for b in held if b > bit)
            low_first = jnp.stack([part, other], axis=axis)
            high_first = jnp.stack([other, part], axis=axis)
            part = jnp.where(rep_bit(bit) == 0, low_first, high_first)
            held.append(bit)
        return part.reshape((nr,) + part.shape[len(held) :])

    return gather(x[:half], first[::-1] + [0]), gather(x[half:], second[::-1] + [0])


def plane_scatter_sum(x, nr):
    bits = bit_count(nr)
    tail = x.shape[1:]
    x = x.reshape((2,) * bits + tail)

    def halve(part, bit, held):
        axis = sum(1 for b in held if b > bit)
        mine = lax.dynamic_index_in_dim(part, rep_bit(bit), axis, keepdims=False)
        other = lax.dynamic_index_in_dim(part, 1 - rep_bit(bit), axis, keepdims=False)
        return mine + xor_swap(other.astype(BF), bit, nr).astype(F32)

    held = list(range(bits))
    x = halve(x, 0, held)
    held.remove(0)
    outs = []
    half = tail[-1] // 2
    for part, order in zip((x[..., :half], x[..., half:]), plane_orders(nr)):
        now = list(held)
        for bit in order:
            part = halve(part, bit, now)
            now.remove(bit)
        outs.append(part)
    return jnp.concatenate(outs, axis=-1)


def plane_sum_small(x, nr):
    for bit in range(bit_count(nr)):
        x = x + xor_swap(x, bit, nr)
    return x


def rotary_tables(length):
    lane = jnp.arange(2 * HEAD_DIM, dtype=jnp.int32) % HEAD_DIM
    half = ROT // 2
    inverse = 10000.0 ** (-(2.0 * (lane % half).astype(F32)) / ROT)
    angles = jnp.arange(length, dtype=jnp.int32).astype(F32)[:, None] * inverse[None, :]
    cosine = jnp.where(lane < ROT, jnp.cos(angles), 1.0)
    sine = jnp.sin(angles)
    from_low = jnp.where((lane >= half) & (lane < ROT), sine, 0.0)
    from_high = jnp.where(lane < half, -sine, 0.0)
    return cosine, from_low, from_high


def turn(x, cosine, from_low, from_high):
    half = ROT // 2
    width = x.shape[1]
    return x * cosine + pltpu.roll(x, half, 1) * from_low + pltpu.roll(x, width - half, 1) * from_high


def attend_kernel(qf_ref, kf_ref, vf_ref, c_ref, lo_ref, hi_ref, q_ref, k_ref, v_ref, p_ref, o_ref):
    length = qf_ref.shape[0]
    cosine, low, high = c_ref[...], lo_ref[...], hi_ref[...]
    q_ref[...] = (turn(qf_ref[...], cosine, low, high).astype(BF).astype(F32) * HEAD_DIM ** (-0.5)).astype(BF)
    k_ref[...] = turn(kf_ref[...], cosine, low, high).astype(BF)
    v_ref[...] = vf_ref[...].astype(BF)
    row = lax.broadcasted_iota(jnp.int32, (QB, QB), 0)
    col = lax.broadcasted_iota(jnp.int32, (QB, QB), 1)
    for h in range(2):
        lanes = slice(h * HEAD_DIM, (h + 1) * HEAD_DIM)
        for i in range(length // QB):
            rows = slice(i * QB, (i + 1) * QB)
            seen = (i + 1) * QB
            s = contract(q_ref[rows, lanes], k_ref[:seen, lanes], 1, 1)
            last = jnp.where(row >= col, s[:, i * QB :], -1e30)
            s = last if i == 0 else jnp.concatenate([s[:, : i * QB], last], axis=1)
            e = jnp.exp(s - jnp.max(s, axis=1, keepdims=True))
            p = (e / jnp.sum(e, axis=1, keepdims=True)).astype(BF)
            p_ref[h, rows, :seen] = p
            o_ref[rows, lanes] = contract(p, v_ref[:seen, lanes], 1, 0).astype(BF)


def attend(projected, tables, width):
    length = projected.shape[0]
    pairs = width // (2 * HEAD_DIM)
    block = (length, 2 * HEAD_DIM)

    def at(third):
        return pl.BlockSpec(block, lambda h: (0, third * pairs + h))

    whole = pl.BlockSpec(block, lambda h: (0, 0))
    mine = pl.BlockSpec(block, lambda h: (0, h))
    piece = jax.ShapeDtypeStruct((length, width), BF)
    return pl.pallas_call(
        attend_kernel,
        grid=(pairs,),
        in_specs=[at(0), at(1), at(2), whole, whole, whole],
        out_specs=[mine, mine, mine, pl.BlockSpec((2, length, length), lambda h: (h, 0, 0)), mine],
        out_shape=[piece, piece, piece, jax.ShapeDtypeStruct((2 * pairs, length, length), BF), piece],
        name="attend",
    )(projected, projected, projected, *tables)


def attend_back_kernel(q_ref, k_ref, v_ref, p_ref, do_ref, c_ref, lo_ref, hi_ref, dq_ref, dk_ref, dv_ref, ds_ref, acc_ref):
    length = q_ref.shape[0]
    blocks = length // QB
    for h in range(2):
        lanes = slice(h * HEAD_DIM, (h + 1) * HEAD_DIM)
        for i in range(blocks):
            rows = slice(i * QB, (i + 1) * QB)
            seen = (i + 1) * QB
            p = p_ref[h, rows, :seen].astype(F32)
            row = lax.broadcasted_iota(jnp.int32, (QB, seen), 0) + i * QB
            col = lax.broadcasted_iota(jnp.int32, (QB, seen), 1)
            p = jnp.where(row >= col, p, 0.0)
            dp = contract(do_ref[rows, lanes], v_ref[:seen, lanes], 1, 1)
            ds = (p * (dp - jnp.sum(p * dp, axis=1, keepdims=True))).astype(BF)
            ds_ref[rows, :seen] = ds
            acc_ref[0, rows, lanes] = contract(ds, k_ref[:seen, lanes], 1, 0) * HEAD_DIM ** (-0.5)
        for j in range(blocks):
            cols = slice(j * QB, (j + 1) * QB)
            rest = slice(j * QB, length)
            acc_ref[1, cols, lanes] = contract(ds_ref[rest, cols], q_ref[rest, lanes], 0, 0)
            acc_ref[2, cols, lanes] = contract(p_ref[h, rest, cols], do_ref[rest, lanes], 0, 0)
    cosine, low, high = c_ref[...], -lo_ref[...], -hi_ref[...]
    dq_ref[...] = turn(acc_ref[0], cosine, low, high).astype(BF)
    dk_ref[...] = turn(acc_ref[1], cosine, low, high).astype(BF)
    dv_ref[...] = acc_ref[2].astype(BF)


def attend_back(q, k, v, probs, d_mixed, tables):
    length, width = q.shape
    pairs = width // (2 * HEAD_DIM)
    block = (length, 2 * HEAD_DIM)
    whole = pl.BlockSpec(block, lambda h: (0, 0))
    mine = pl.BlockSpec(block, lambda h: (0, h))
    piece = jax.ShapeDtypeStruct((length, width), BF)
    return pl.pallas_call(
        attend_back_kernel,
        grid=(pairs,),
        in_specs=[mine, mine, mine, pl.BlockSpec((2, length, length), lambda h: (h, 0, 0)), mine, whole, whole, whole],
        out_specs=[mine, mine, mine],
        out_shape=[piece, piece, piece],
        scratch_shapes=[pltpu.VMEM((length, length), BF), pltpu.VMEM((3,) + block, F32)],
        name="attend_back",
    )(q, k, v, probs, d_mixed, *tables)


def split(x):
    high = x.astype(BF)
    return high, (x - high.astype(F32)).astype(BF)


def ortho_kernel(g_ref, s_ref, x_ref, gh, gl, th, tl, pm):
    size = g_ref.shape[0]
    step = min(256, size)
    parts = [slice(i * step, (i + 1) * step) for i in range(size // step)]
    width = x_ref.shape[0]
    trace = jnp.zeros((), F32)
    row = lax.broadcasted_iota(jnp.int32, (step, step), 0)
    col = lax.broadcasted_iota(jnp.int32, (step, step), 1)
    for part in parts:
        trace = trace + jnp.sum(jnp.where(row == col, g_ref[part, part], 0.0))
    scale = 1.0 / (jnp.sqrt(jnp.broadcast_to(trace, (1, 1))) + 1e-07)
    for part in parts:
        gh[part], gl[part] = split(g_ref[part] * (scale * scale))
    x_ref[...] = (s_ref[...].astype(F32) * scale).astype(BF)

    def poly():
        for part in parts:
            square = contract(gh[part], gh[...], 1, 0)
            pm[part] = (COEF_B * gh[part].astype(F32) + COEF_C * square).astype(BF)

    def advance():
        x = x_ref[...]
        x_ref[...] = (COEF_A * x.astype(F32) + contract(x, pm[...], 1, 0)).astype(BF)

    def body(_, carry):
        poly()
        advance()
        for part in parts:
            left = pm[part]
            total = COEF_A * (gh[part].astype(F32) + gl[part].astype(F32))
            total = total + contract(left, gh[...], 1, 0) + contract(left, gl[...], 1, 0)
            th[part], tl[part] = split(total)
        for part in parts:
            total = COEF_A * (th[part].astype(F32) + tl[part].astype(F32))
            total = total + contract(th[part], pm[...], 1, 0) + contract(tl[part], pm[...], 1, 0)
            gh[part], gl[part] = split(total)
        return carry

    lax.fori_loop(0, NS - 1, body, 0)
    poly()
    advance()


def orthogonalize(gram, rows):
    size = gram.shape[0]
    square = pltpu.VMEM((size, size), BF)
    return pl.pallas_call(
        ortho_kernel,
        in_specs=[pl.BlockSpec(memory_space=pltpu.VMEM)] * 2,
        out_specs=pl.BlockSpec(memory_space=pltpu.VMEM),
        out_shape=jax.ShapeDtypeStruct(rows.shape, BF),
        scratch_shapes=[square] * 5,
        name="orthogonalize",
    )(gram, rows)


def layer_norm_parts(values):
    center = values - jnp.mean(values, axis=-1, keepdims=True)
    spread = jnp.mean(center * center, axis=-1, keepdims=True)
    scale = lax.rsqrt(spread + 1e-05)
    return center * scale, scale


def gelu_tanh(values):
    return jax.nn.gelu(values, approximate=True)


def on_device(
    tokens,
    cotangent,
    qkv_weight,
    out_weight,
    up_weight,
    down_weight,
    ln_gain,
    ln_bias,
    up_bias,
    down_bias,
    qkv_moment,
    out_moment,
    up_moment,
    down_moment,
    gain_moment,
    beta_moment,
    up_bias_moment,
    down_bias_moment,
):
    nf = lax.axis_size("fsdp")
    nr = lax.axis_size("rep")
    f = lax.axis_index("fsdp")
    r = lax.axis_index("rep")
    _, local_len, width = tokens.shape
    rows = qkv_weight.shape[0]
    hidden_width = up_weight.shape[1] // nf
    head_width = width // nf
    unit = hidden_width // nr
    qkv_units = 3 * nr // 4

    tok = tokens.reshape(local_len, width)
    cot = cotangent.reshape(local_len, width)

    def by_dest(weight, thirds):
        parts = weight.reshape(rows, thirds, nf, -1)
        return parts.transpose(2, 0, 1, 3).reshape(nf, rows, -1)

    cols = jnp.concatenate([by_dest(qkv_weight, 3), by_dest(up_weight, 1), by_dest(down_weight, 1)], axis=2)
    share = rows // nr
    cols = lax.dynamic_slice_in_dim(cols, r * share, share, 1)
    got = z_exchange(cols)
    total_cols = got.shape[2]
    half_a, half_b = plane_gather(got, nr)
    gathered = jnp.concatenate([half_a, half_b], axis=1)
    slab = gathered.transpose(1, 0, 2, 3).reshape(width, total_cols)
    qkv_cols = slab[:, : 3 * head_width]
    up_cols = slab[:, 3 * head_width : 3 * head_width + hidden_width]
    down_cols = slab[:, 3 * head_width + hidden_width :]

    vectors = z_gather(jnp.stack([ln_gain, ln_bias, down_bias]).reshape(1, 3 * rows), nf)
    vectors = vectors.reshape(nf, 3, rows).transpose(1, 0, 2).reshape(3, width).astype(F32)
    gain, beta, down_bias_full = vectors[0], vectors[1], vectors[2]

    tok_all = z_gather(tok, nf)
    cot_all = z_gather(cot, nf)
    length = tok_all.shape[0]
    xhat_all, _ = layer_norm_parts(tok_all.astype(F32))
    normed = (xhat_all * gain + beta).astype(BF)

    projected = jnp.dot(normed, qkv_cols, preferred_element_type=F32)
    tables = rotary_tables(length)
    q, k, v, probs, mixed = attend(projected, tables, head_width)
    hidden_pre = jnp.dot(normed, up_cols, preferred_element_type=F32) + up_bias.astype(F32)
    hidden_f, gelu_pull = jax.vjp(gelu_tanh, hidden_pre)
    hidden = hidden_f.astype(BF)
    partial_out = jnp.dot(mixed, out_weight, preferred_element_type=F32) + contract(hidden, down_cols, 1, 1)

    d_hidden = jnp.dot(cot_all, down_cols, preferred_element_type=F32)
    d_pre = gelu_pull(d_hidden)[0].astype(BF)
    d_mixed = contract(cot_all, out_weight, 1, 1).astype(BF)
    dq, dk, dv = attend_back(q, k, v, probs, d_mixed, tables)
    d_projected = jnp.concatenate([dq, dk, dv], axis=1)
    partial_normed = contract(d_projected, qkv_cols, 1, 1) + contract(d_pre, up_cols, 1, 1)

    grad_up = contract(d_pre, normed, 0, 0)
    grad_down = contract(hidden, cot_all, 0, 0)
    grad_comb = jnp.concatenate([contract(d_projected, normed, 0, 0), contract(mixed, cot_all, 0, 0)], axis=0)

    def scatter(grad):
        return plane_scatter_sum(grad.reshape(nr, unit, width), nr)

    unit_up, unit_down, unit_comb = scatter(grad_up), scatter(grad_down), scatter(grad_comb)
    units = (unit_comb, unit_up, unit_down)
    is_out = r >= qkv_units

    def unit_columns(moment, thirds):
        parts = moment.reshape(rows, thirds, nf, -1).transpose(2, 1, 3, 0)
        parts = parts.reshape(nf, -1, rows)
        start = jnp.minimum(r, parts.shape[1] // unit - 1) * unit
        return lax.dynamic_slice_in_dim(parts, start, unit, 1).reshape(nf * unit, rows)

    out_start = jnp.maximum(r - qkv_units, 0) * unit
    out_rows = lax.dynamic_slice_in_dim(out_moment, out_start, unit, 0)
    out_rows = out_rows.reshape(unit, nf, rows).transpose(1, 0, 2).reshape(nf * unit, rows)
    owned = [unit_columns(qkv_moment, 3), out_rows, unit_columns(up_moment, 1), unit_columns(down_moment, 1)]
    owned = [(MOMENTUM_RATE * m).astype(BF) for m in owned]
    owned = owned + [jnp.zeros((nf * unit, rows), BF)] * (nf - 4)
    moment_in = z_exchange(jnp.stack(owned)).reshape(nf, nf, unit, rows)
    out_plane = is_out & (f == 1)
    moment_rows = jnp.where(
        out_plane, moment_in.transpose(0, 2, 1, 3), moment_in.transpose(1, 2, 0, 3)
    ).reshape(nf * unit, width)

    sends = [unit_comb, unit_comb, unit_up, unit_down]
    sends = [s.astype(BF) for s in sends] + [jnp.zeros((unit, width), BF)] * (nf - 4)
    grad_rows = z_exchange(jnp.stack(sends)).reshape(nf * unit, width)
    active = jnp.where(f == 0, ~is_out, jnp.where(f == 1, is_out, f < 4))
    s_rows = jnp.where(active, moment_rows.astype(F32) + grad_rows.astype(F32), 0.0).astype(BF)

    s_a, s_b = plane_gather(s_rows, nr)
    s_all = jnp.concatenate([s_a, s_b], axis=1).reshape(nr * nf * unit, width)
    gram = contract(s_all, s_all, 0, 0)
    ortho = orthogonalize(gram, s_rows)

    blocks = ortho.reshape(nf, unit, nf, rows)
    back = jnp.where(out_plane, blocks.transpose(0, 2, 1, 3), blocks.transpose(2, 0, 1, 3))
    back = z_exchange(back).reshape(nf, nf * unit, rows)
    ortho_mine = jnp.stack([jnp.where(is_out, back[1], back[0]), back[2], back[3]])

    grad_send = jnp.stack([u.astype(BF).reshape(unit, nf, rows).transpose(1, 0, 2) for u in units], axis=1)
    grad_got = z_exchange(grad_send)
    kept = jnp.where(is_out, grad_send[:, 0], grad_got[:, 0])
    grad_mine = jnp.stack([kept, grad_got[:, 1], grad_got[:, 2]]).reshape(3, nf * unit, rows)

    def spread(mine):
        a, b = plane_gather(mine.transpose(1, 0, 2), nr)
        whole = jnp.concatenate([a, b], axis=1).reshape(nr, nf, unit, 3, rows)
        qkv = whole[:qkv_units, :, :, 0].reshape(3, qkv_units // 3, nf, unit, rows)
        qkv = qkv.transpose(4, 0, 2, 1, 3).reshape(rows, 3 * width)
        out = whole[qkv_units:, :, :, 0].transpose(0, 2, 1, 3).reshape(rows, width)
        up = whole[:, :, :, 1].transpose(3, 1, 0, 2).reshape(rows, -1)
        down = whole[:, :, :, 2].transpose(3, 1, 0, 2).reshape(rows, -1)
        return [m.astype(F32) for m in (qkv, out, up, down)]

    grads = spread(grad_mine)
    orthos = spread(ortho_mine)
    mats = (qkv_weight, out_weight, up_weight, down_weight)
    moments = (qkv_moment, out_moment, up_moment, down_moment)
    new_moments = [MOMENTUM_RATE * m + g for m, g in zip(moments, grads)]
    new_mats = [
        w.astype(F32) - MATRIX_RATE * 0.2 * math.sqrt(w.shape[1]) * o for w, o in zip(mats, orthos)
    ]

    summed = z_scatter_sum(partial_out.reshape(nf, local_len, width), nf)
    inputs = tok.astype(F32)
    block_out = (inputs + summed + down_bias_full).astype(BF)
    d_normed = z_scatter_sum(partial_normed.reshape(nf, local_len, width), nf)
    xhat, inv_std = layer_norm_parts(inputs)
    e = d_normed * gain
    input_grad = cot.astype(F32) + inv_std * (
        e - jnp.mean(e, axis=-1, keepdims=True) - xhat * jnp.mean(e * xhat, axis=-1, keepdims=True)
    )

    pair = jnp.stack([jnp.sum(d_normed * xhat, axis=0), jnp.sum(d_normed, axis=0)])
    pair = pair.reshape(2, nf, rows).transpose(1, 0, 2)
    pair = jnp.sum(z_exchange(pair), axis=0).reshape(2 * rows)
    down_sum = jnp.sum(lax.dynamic_slice_in_dim(cot_all, f * rows, rows, 1).astype(F32), axis=0)
    up_sum = jnp.sum(d_pre.astype(F32), axis=0)
    small = plane_sum_small(jnp.concatenate([pair, down_sum, up_sum]), nr)
    vec_grads = [small[:rows], small[rows : 2 * rows], small[3 * rows :], small[2 * rows : 3 * rows]]
    vec_moments = [
        MOMENTUM_RATE * m + g
        for m, g in zip((gain_moment, beta_moment, up_bias_moment, down_bias_moment), vec_grads)
    ]
    vec_new = [
        p.astype(F32) - VECTOR_RATE * m for p, m in zip((ln_gain, ln_bias, up_bias, down_bias), vec_moments)
    ]

    return (
        block_out.reshape(1, local_len, width),
        input_grad.reshape(1, local_len, width),
        *grads,
        *vec_grads,
        *new_mats,
        *vec_new,
        *new_moments,
        *vec_moments,
    )


def solution(mesh):
    split3 = P("rep", "fsdp", None)
    mat = P("fsdp", None)
    vec = P("fsdp")
    return jax.shard_map(
        on_device,
        mesh=mesh,
        in_specs=(split3,) * 2 + (mat,) * 4 + (vec,) * 4 + (mat,) * 4 + (vec,) * 4,
        out_specs=(split3,) * 2 + ((mat,) * 4 + (vec,) * 4) * 3,
        check_vma=False,
    )
```

```python
import math

import jax
import jax.numpy as jnp
from jax import lax
from jax.experimental import pallas as pl
from jax.experimental.pallas import tpu as pltpu
from jax.sharding import PartitionSpec as P


HEAD_DIM = 64
ROT = 32
NS = 5
QB = 256

MOMENTUM_RATE = 0.9
MATRIX_RATE = 0.05
VECTOR_RATE = 0.002
COEF_A = 3.4445
COEF_B = -4.775
COEF_C = 2.0315

BF = jnp.bfloat16
F32 = jnp.float32


def contract(left, right, left_dim, right_dim):
    return lax.dot_general(
        left, right, (((left_dim,), (right_dim,)), ((), ())), preferred_element_type=F32
    )


def after(x, *others):
    return lax.optimization_barrier((x,) + others)[0]


def z_neighbours(x, nf):
    right = lax.ppermute(x, "fsdp", [(i, i + 1) for i in range(nf - 1)])
    left = lax.ppermute(x, "fsdp", [(i, i - 1) for i in range(1, nf)])
    return right, left


def z_gather(x, near, nf):
    f = lax.axis_index("fsdp")
    length = x.shape[0]
    right, left = near
    from_left, from_right = [right], [left]
    for step in range(1, nf - 1):
        from_left.append(lax.ppermute(right, "fsdp", [(i, i + step) for i in range(1, nf - step)]))
        from_right.append(lax.ppermute(left, "fsdp", [(i, i - step) for i in range(step, nf - 1)]))
    line = jnp.concatenate(from_left[::-1] + [x] + from_right, axis=0)
    return lax.dynamic_slice_in_dim(line, (nf - 1 - f) * length, nf * length, 0)


def z_exchange(x):
    return lax.all_to_all(x, "fsdp", split_axis=0, concat_axis=0, tiled=True)


def xor_swap(x, mask, nr):
    return lax.ppermute(x, "rep", [(i, i ^ mask) for i in range(nr)])


def rep_bit(bit):
    return (lax.axis_index("rep") >> bit) & 1


def high_bits(nr):
    return list(range(1, nr.bit_length() - 1))


def place(index, nr):
    return (index & 1) * (nr // 2) + (index >> 1)


def plane_pieces(x, axis, nr):
    order = high_bits(nr)
    middle = x.shape[axis] // 2

    def halves(part):
        return lax.slice_in_dim(part, 0, middle, axis=axis), lax.slice_in_dim(part, middle, 2 * middle, axis=axis)

    if len(order) == 2:
        one, two = 1 << order[0], 1 << order[1]
        near, far = xor_swap(x, one, nr), xor_swap(x, two, nr)
        both = (xor_swap(halves(far)[0], one, nr), xor_swap(halves(near)[1], two, nr))
        return {0: (x,), one: (near,), two: (far,), one | two: both}
    sides = []
    for part, bits in zip(halves(x), (order[::-1], order)):
        held = {0: part}
        for bit in bits:
            for distance in list(held):
                held[distance | (1 << bit)] = xor_swap(held[distance], 1 << bit, nr)
        sides.append(held)
    return {distance: (sides[0][distance], sides[1][distance]) for distance in sides[0]}


def with_partner(pieces, nr):
    found = dict(pieces)
    for distance, parts in pieces.items():
        found[distance | 1] = tuple(xor_swap(part, 1, nr) for part in parts)
    return found


def listed(pieces):
    return [(d, n, len(pieces[d]), part) for d in sorted(pieces) for n, part in enumerate(pieces[d])]


def halve(x, axis, bit, nr):
    mine = lax.dynamic_index_in_dim(x, rep_bit(bit), axis, keepdims=False)
    other = lax.dynamic_index_in_dim(x, 1 - rep_bit(bit), axis, keepdims=False)
    return mine + xor_swap(other.astype(BF), 1 << bit, nr).astype(F32)


def plane_sum(x, order, nr):
    held = high_bits(nr)
    x = x.reshape((2,) * len(held) + x.shape[1:])
    for bit in order:
        x = halve(x, sum(1 for b in held if b > bit), bit, nr)
        held.remove(bit)
    return x


def plane_sum_small(x, nr):
    for bit in range(nr.bit_length() - 1):
        x = x + xor_swap(x, 1 << bit, nr)
    return x


def rotary_tables(length):
    lane = jnp.arange(2 * HEAD_DIM, dtype=jnp.int32) % HEAD_DIM
    half = ROT // 2
    inverse = 10000.0 ** (-(2.0 * (lane % half).astype(F32)) / ROT)
    angles = jnp.arange(length, dtype=jnp.int32).astype(F32)[:, None] * inverse[None, :]
    cosine = jnp.where(lane < ROT, jnp.cos(angles), 1.0)
    sine = jnp.sin(angles)
    from_low = jnp.where((lane >= half) & (lane < ROT), sine, 0.0)
    from_high = jnp.where(lane < half, -sine, 0.0)
    return cosine, from_low, from_high


def turn(x, cosine, from_low, from_high):
    half = ROT // 2
    width = x.shape[1]
    return x * cosine + pltpu.roll(x, half, 1) * from_low + pltpu.roll(x, width - half, 1) * from_high


def attend_kernel(qf_ref, kf_ref, vf_ref, c_ref, lo_ref, hi_ref, q_ref, k_ref, v_ref, p_ref, o_ref):
    length = qf_ref.shape[0]
    cosine, low, high = c_ref[...], lo_ref[...], hi_ref[...]
    q_ref[...] = (turn(qf_ref[...], cosine, low, high).astype(BF).astype(F32) * HEAD_DIM ** (-0.5)).astype(BF)
    k_ref[...] = turn(kf_ref[...], cosine, low, high).astype(BF)
    v_ref[...] = vf_ref[...].astype(BF)
    row = lax.broadcasted_iota(jnp.int32, (QB, QB), 0)
    col = lax.broadcasted_iota(jnp.int32, (QB, QB), 1)
    for h in range(2):
        lanes = slice(h * HEAD_DIM, (h + 1) * HEAD_DIM)
        for i in range(length // QB):
            rows = slice(i * QB, (i + 1) * QB)
            seen = (i + 1) * QB
            s = contract(q_ref[rows, lanes], k_ref[:seen, lanes], 1, 1)
            last = jnp.where(row >= col, s[:, i * QB :], -1e30)
            s = last if i == 0 else jnp.concatenate([s[:, : i * QB], last], axis=1)
            e = jnp.exp(s - jnp.max(s, axis=1, keepdims=True))
            p = (e / jnp.sum(e, axis=1, keepdims=True)).astype(BF)
            p_ref[h, rows, :seen] = p
            o_ref[rows, lanes] = contract(p, v_ref[:seen, lanes], 1, 0).astype(BF)


def attend(projected, tables, width):
    length = projected.shape[0]
    pairs = width // (2 * HEAD_DIM)
    block = (length, 2 * HEAD_DIM)

    def at(third):
        return pl.BlockSpec(block, lambda h: (0, third * pairs + h))

    whole = pl.BlockSpec(block, lambda h: (0, 0))
    mine = pl.BlockSpec(block, lambda h: (0, h))
    piece = jax.ShapeDtypeStruct((length, width), BF)
    return pl.pallas_call(
        attend_kernel,
        grid=(pairs,),
        in_specs=[at(0), at(1), at(2), whole, whole, whole],
        out_specs=[mine, mine, mine, pl.BlockSpec((2, length, length), lambda h: (h, 0, 0)), mine],
        out_shape=[piece, piece, piece, jax.ShapeDtypeStruct((2 * pairs, length, length), BF), piece],
        name="attend",
    )(projected, projected, projected, *tables)


def attend_back_kernel(q_ref, k_ref, v_ref, p_ref, do_ref, c_ref, lo_ref, hi_ref, dq_ref, dk_ref, dv_ref, ds_ref, acc_ref):
    length = q_ref.shape[0]
    blocks = length // QB
    for h in range(2):
        lanes = slice(h * HEAD_DIM, (h + 1) * HEAD_DIM)
        for i in range(blocks):
            rows = slice(i * QB, (i + 1) * QB)
            seen = (i + 1) * QB
            p = p_ref[h, rows, :seen].astype(F32)
            row = lax.broadcasted_iota(jnp.int32, (QB, seen), 0) + i * QB
            col = lax.broadcasted_iota(jnp.int32, (QB, seen), 1)
            p = jnp.where(row >= col, p, 0.0)
            dp = contract(do_ref[rows, lanes], v_ref[:seen, lanes], 1, 1)
            ds = (p * (dp - jnp.sum(p * dp, axis=1, keepdims=True))).astype(BF)
            ds_ref[rows, :seen] = ds
            acc_ref[0, rows, lanes] = contract(ds, k_ref[:seen, lanes], 1, 0) * HEAD_DIM ** (-0.5)
        for j in range(blocks):
            cols = slice(j * QB, (j + 1) * QB)
            rest = slice(j * QB, length)
            acc_ref[1, cols, lanes] = contract(ds_ref[rest, cols], q_ref[rest, lanes], 0, 0)
            acc_ref[2, cols, lanes] = contract(p_ref[h, rest, cols], do_ref[rest, lanes], 0, 0)
    cosine, low, high = c_ref[...], -lo_ref[...], -hi_ref[...]
    dq_ref[...] = turn(acc_ref[0], cosine, low, high).astype(BF)
    dk_ref[...] = turn(acc_ref[1], cosine, low, high).astype(BF)
    dv_ref[...] = acc_ref[2].astype(BF)


def attend_back(q, k, v, probs, d_mixed, tables):
    length, width = q.shape
    pairs = width // (2 * HEAD_DIM)
    block = (length, 2 * HEAD_DIM)
    whole = pl.BlockSpec(block, lambda h: (0, 0))
    mine = pl.BlockSpec(block, lambda h: (0, h))
    piece = jax.ShapeDtypeStruct((length, width), BF)
    return pl.pallas_call(
        attend_back_kernel,
        grid=(pairs,),
        in_specs=[mine, mine, mine, pl.BlockSpec((2, length, length), lambda h: (h, 0, 0)), mine, whole, whole, whole],
        out_specs=[mine, mine, mine],
        out_shape=[piece, piece, piece],
        scratch_shapes=[pltpu.VMEM((length, length), BF), pltpu.VMEM((3,) + block, F32)],
        name="attend_back",
    )(q, k, v, probs, d_mixed, *tables)


def split(x):
    high = x.astype(BF)
    return high, (x - high.astype(F32)).astype(BF)


def upper(count):
    return [(i, j) for i in range(count) for j in range(i, count)]


def gram_of(pieces):
    entries = listed(pieces)
    slots = sorted(pieces)
    size = sum(part.shape[0] for part in pieces[0])
    wide = pieces[0][0].shape[1]
    count = size // QB

    def kernel(*refs):
        ins, out, slab, sems = refs[:-3], refs[-3], refs[-2], refs[-1]
        copies = []
        for k, (d, n, _, part) in enumerate(entries):
            rows = part.shape[0]
            to = slab.at[pl.ds(n * rows, rows), pl.ds(slots.index(d) * wide, wide)]
            copies.append(pltpu.make_async_copy(ins[k], to, sems.at[k]))
        for copy in copies:
            copy.start()
        for copy in copies:
            copy.wait()
        for i in range(count):
            strip = contract(slab[i * QB : (i + 1) * QB], slab[i * QB :], 1, 1)
            for j in range(i, count):
                out[upper(count).index((i, j))] = strip[:, (j - i) * QB : (j - i + 1) * QB]

    return pl.pallas_call(
        kernel,
        in_specs=[pl.BlockSpec(memory_space=pl.ANY)] * len(entries),
        out_specs=pl.BlockSpec(memory_space=pltpu.VMEM),
        out_shape=jax.ShapeDtypeStruct((count * (count + 1) // 2, QB, QB), F32),
        scratch_shapes=[
            pltpu.VMEM((size, wide * len(slots)), BF),
            pltpu.SemaphoreType.DMA((len(entries),)),
        ],
        cost_estimate=pl.CostEstimate(
            flops=2 * size * size * wide * len(slots), transcendentals=0, bytes_accessed=2 * size * wide * len(slots)
        ),
        name="gram",
    )(*[part for _, _, _, part in entries])


def ortho_kernel(flag_ref, ga_ref, gb_ref, s_ref, out_ref, x_ref, gh, gl, th, tl, pm):
    size = gh.shape[0]
    count = size // QB
    parts = [slice(i * QB, (i + 1) * QB) for i in range(count)]
    pairs = upper(count)
    trace = jnp.zeros((), F32)
    row = lax.broadcasted_iota(jnp.int32, (QB, QB), 0)
    col = lax.broadcasted_iota(jnp.int32, (QB, QB), 1)
    for i in range(count):
        n = pairs.index((i, i))
        trace = trace + jnp.sum(jnp.where(row == col, ga_ref[n] + gb_ref[n], 0.0))
    scale = 1.0 / (jnp.sqrt(jnp.broadcast_to(trace, (1, 1))) + 1e-07)

    def put(i, j, block):
        high, low = split(block)
        gh[parts[i], parts[j]], gl[parts[i], parts[j]] = high, low
        if i != j:
            turned = block.T
            high, low = split(turned)
            gh[parts[j], parts[i]], gl[parts[j], parts[i]] = high, low

    for n, (i, j) in enumerate(pairs):
        put(i, j, (ga_ref[n] + gb_ref[n]) * (scale * scale))
    x_ref[...] = (s_ref[...].astype(F32) * scale).astype(BF)

    def poly():
        for i in range(count):
            rest = slice(i * QB, size)
            square = contract(gh[parts[i]], gh[:, rest], 1, 0)
            block = COEF_B * gh[parts[i], rest].astype(F32) + COEF_C * square
            pm[parts[i], rest] = block.astype(BF)
            for j in range(i + 1, count):
                pm[parts[j], parts[i]] = block[:, (j - i) * QB : (j - i + 1) * QB].T.astype(BF)

    def advance():
        x = x_ref[...]
        x_ref[...] = (COEF_A * x.astype(F32) + contract(pm[...], x, 1, 0)).astype(BF)

    def body(_, carry):
        poly()
        advance()
        for part in parts:
            left = pm[part]
            total = COEF_A * (gh[part].astype(F32) + gl[part].astype(F32))
            total = total + contract(left, gh[...], 1, 0) + contract(left, gl[...], 1, 0)
            th[part], tl[part] = split(total)
        for i in range(count):
            rest = slice(i * QB, size)
            total = COEF_A * (th[parts[i], rest].astype(F32) + tl[parts[i], rest].astype(F32))
            total = total + contract(th[parts[i]], pm[:, rest], 1, 0) + contract(tl[parts[i]], pm[:, rest], 1, 0)
            for j in range(i, count):
                put(i, j, total[:, (j - i) * QB : (j - i + 1) * QB])
        return carry

    lax.fori_loop(0, NS - 1, body, 0)
    poly()
    advance()
    nf, wide, _ = out_ref.shape
    unit = x_ref.shape[1] // nf

    @pl.when(flag_ref[0] == 0)
    def _():
        for a in range(nf):
            out_ref[a] = x_ref[a * wide : (a + 1) * wide]

    @pl.when(flag_ref[0] == 1)
    def _():
        for a in range(nf):
            for b in range(nf):
                out_ref[b, :, a * unit : (a + 1) * unit] = x_ref[a * wide : (a + 1) * wide, b * unit : (b + 1) * unit]


def orthogonalize(swapped, gram_a, gram_b, cols, nf):
    size = cols.shape[0]
    square = pltpu.VMEM((size, size), BF)
    vmem = pl.BlockSpec(memory_space=pltpu.VMEM)
    return pl.pallas_call(
        ortho_kernel,
        in_specs=[pl.BlockSpec(memory_space=pltpu.SMEM), vmem, vmem, vmem],
        out_specs=vmem,
        out_shape=jax.ShapeDtypeStruct((nf, size // nf, cols.shape[1]), BF),
        scratch_shapes=[pltpu.VMEM(cols.shape, BF)] + [square] * 5,
        cost_estimate=pl.CostEstimate(
            flops=40 * size**3, transcendentals=0, bytes_accessed=8 * size * size
        ),
        name="orthogonalize",
    )(swapped.astype(jnp.int32).reshape(1), gram_a, gram_b, cols)


def momentum_cols(active, moment, grads):
    nf, size, unit = grads.shape

    def kernel(flag_ref, m_ref, g_ref, out_ref):
        keep = jnp.full((size, unit), flag_ref[0], jnp.int32) == 1
        for b in range(nf):
            lanes = slice(b * unit, (b + 1) * unit)
            total = m_ref[:, lanes].astype(F32) + g_ref[b].astype(F32)
            out_ref[:, lanes] = jnp.where(keep, total, 0.0).astype(BF)

    vmem = pl.BlockSpec(memory_space=pltpu.VMEM)
    return pl.pallas_call(
        kernel,
        in_specs=[pl.BlockSpec(memory_space=pltpu.SMEM), vmem, vmem],
        out_specs=vmem,
        out_shape=jax.ShapeDtypeStruct(moment.shape, BF),
        name="momentum_cols",
    )(active.astype(jnp.int32).reshape(1), moment, grads)


def rep_scalar():
    return lax.axis_index("rep").astype(jnp.int32).reshape(1)


def assemble(pieces, nr):
    entries = listed(pieces)
    count = sum(part.shape[0] for part in pieces[0])
    tail = pieces[0][0].shape[1:]

    def kernel(r_ref, *refs):
        ins, out, sems = refs[:-2], refs[-2], refs[-1]
        copies = []
        for k, (d, n, _, part) in enumerate(entries):
            to = out.at[pl.ds(n * part.shape[0], part.shape[0]), r_ref[0] ^ d]
            copies.append(pltpu.make_async_copy(ins[k], to, sems.at[k]))
        for copy in copies:
            copy.start()
        for copy in copies:
            copy.wait()

    return pl.pallas_call(
        kernel,
        in_specs=[pl.BlockSpec(memory_space=pltpu.SMEM)] + [pl.BlockSpec(memory_space=pl.ANY)] * len(entries),
        out_specs=pl.BlockSpec(memory_space=pltpu.VMEM),
        out_shape=jax.ShapeDtypeStruct((count, nr) + tail, pieces[0][0].dtype),
        scratch_shapes=[pltpu.SemaphoreType.DMA((len(entries),))],
    )(rep_scalar(), *[part for _, _, _, part in entries])


def grad_mlp(which, d_pre, normed, hidden, cot, blocks, dtype):
    length, width = normed.shape
    mid = d_pre.shape[1] // 2
    step = min(mid, QB)
    count = mid // step
    unit = mid // blocks

    def kernel(w_ref, a_ref, x_ref, b_ref, y_ref, out_ref):
        def put(left, right):
            out_ref[0] = contract(left[...], right[...], 0, 0).reshape(step // unit, unit, width).astype(dtype)

        @pl.when(pl.program_id(0) == 0)
        def _():
            put(a_ref, x_ref)

        @pl.when(pl.program_id(0) == 1)
        def _():
            put(b_ref, y_ref)

    whole = pl.BlockSpec((length, width), lambda m, i, w: (0, 0))
    return pl.pallas_call(
        kernel,
        grid_spec=pltpu.PrefetchScalarGridSpec(
            num_scalar_prefetch=1,
            grid=(2, count),
            in_specs=[
                pl.BlockSpec((length, step), lambda m, i, w: (0, w[0] * count + jnp.where(m == 0, i, count - 1))),
                whole,
                pl.BlockSpec((length, step), lambda m, i, w: (0, w[0] * count + jnp.where(m == 1, i, 0))),
                whole,
            ],
            out_specs=pl.BlockSpec((1, step // unit, unit, width), lambda m, i, w: (m, i, 0, 0)),
        ),
        out_shape=jax.ShapeDtypeStruct((2, blocks, unit, width), dtype),
        cost_estimate=pl.CostEstimate(
            flops=4 * length * mid * width, transcendentals=0, bytes_accessed=8 * length * width
        ),
        name="grad_mlp",
    )(which.astype(jnp.int32).reshape(1), d_pre, normed, hidden, cot)


def grad_comb(which, dq, dk, dv, mixed, normed, cot, blocks, dtype):
    length, width = normed.shape
    step = dq.shape[1]
    unit = 2 * step // blocks

    def kernel(w_ref, q_ref, k_ref, v_ref, m_ref, x_ref, y_ref, out_ref):
        def put(left, right):
            out_ref[...] = contract(left[...], right[...], 0, 0).reshape(step // unit, unit, width).astype(dtype)

        at = 2 * w_ref[0] + pl.program_id(0)
        for n, (left, right) in enumerate(((q_ref, x_ref), (k_ref, x_ref), (v_ref, x_ref), (m_ref, y_ref))):

            @pl.when(at == n)
            def _(left=left, right=right):
                put(left, right)

    left = pl.BlockSpec((length, step), lambda i, w: (0, 0))
    whole = pl.BlockSpec((length, width), lambda i, w: (0, 0))
    return pl.pallas_call(
        kernel,
        grid_spec=pltpu.PrefetchScalarGridSpec(
            num_scalar_prefetch=1,
            grid=(2,),
            in_specs=[left] * 4 + [whole] * 2,
            out_specs=pl.BlockSpec((step // unit, unit, width), lambda i, w: (i, 0, 0)),
        ),
        out_shape=jax.ShapeDtypeStruct((blocks, unit, width), dtype),
        cost_estimate=pl.CostEstimate(
            flops=4 * length * step * width, transcendentals=0, bytes_accessed=8 * length * width
        ),
        name="grad_comb",
    )(which.astype(jnp.int32).reshape(1), dq, dk, dv, mixed, normed, cot)


def grad_rule(block, have):
    return block, MOMENTUM_RATE * have + block


def weight_rule(step):
    def rule(block, have):
        return (have.astype(F32) - step * block,)

    return rule


def finish_plain(pieces, have, rules, nr):
    whole = jnp.stack([jnp.concatenate(pieces[d], axis=1) for d in sorted(pieces)])
    index = jnp.arange(nr)
    source = (index // (nr // 2)) | ((index % (nr // 2)) << 1)
    whole = whole[source ^ lax.axis_index("rep")]
    per = nr // 4
    rows = whole.shape[2]
    nf = have[1].shape[1] // rows
    whole = whole.reshape(nr, 3, rows, nf, -1)
    unit = whole.shape[4]
    qkv = whole[: 3 * per, 0].reshape(3, per, rows, nf, unit).transpose(2, 0, 3, 1, 4).reshape(rows, -1)
    out = whole[3 * per :, 0].transpose(0, 3, 2, 1).reshape(rows, -1)
    up = whole[:, 1].transpose(1, 2, 0, 3).reshape(rows, -1)
    down = whole[:, 2].transpose(1, 2, 0, 3).reshape(rows, -1)
    return [rule(m.astype(F32), x) for m, x, rule in zip((qkv, out, up, down), have, rules)]


def finish(pieces, have, rules, outs, nr):
    entries = listed(pieces)
    parts = [part for _, _, _, part in entries]
    wide = parts[0].shape[2]
    rows = sum(part.shape[1] for part in pieces[0])
    nf = have[1].shape[1] // rows
    u = wide // nf
    if u % 128:
        return finish_plain(pieces, have, rules, nr)
    per = nr // 4
    order = [(2, 1, nf), (3, 2, nf), (0, 0, 3), (1, 0, 1)]
    starts = [0, nf, 2 * nf, 2 * nf + 3]
    steps = 2 * nf + 4

    def kernel(r_ref, *refs):
        ins = refs[: len(parts)]
        have_refs = refs[len(parts) : len(parts) + 4]
        out_refs = refs[len(parts) + 4 : len(parts) + 4 + 4 * outs]
        slab, sems = refs[-2:]
        step = pl.program_id(0)

        def copies(which):
            for k, (d, n, _, part) in enumerate(entries):
                to = slab.at[place(r_ref[0] ^ d, nr), which, pl.ds(n * part.shape[1], part.shape[1])]
                yield pltpu.make_async_copy(ins[k].at[which], to, sems.at[k, which])

        @pl.when(step == 0)
        def _():
            for which in (1, 2, 0):
                for copy in copies(which):
                    copy.start()

        def write(matrix, at, block):
            values = rules[matrix](block.astype(F32), have_refs[matrix][at])
            for n, value in enumerate(values):
                out_refs[matrix * outs + n][at] = value

        for (matrix, which, count), start in zip(order, starts):
            for k in range(count):

                @pl.when(step == start + k)
                def _(matrix=matrix, which=which, start=start, k=k):
                    if k == 0 and matrix != 1:
                        for copy in copies(which):
                            copy.wait()
                    if matrix >= 2:
                        for p in range(nr):
                            at = (slice(None), slice(p * u, (p + 1) * u))
                            write(matrix, at, slab[p, which, :, k * u : (k + 1) * u])
                    elif matrix == 0:
                        for b in range(nf):
                            for s in range(per):
                                at = (slice(None), slice((b * per + s) * u, (b * per + s + 1) * u))
                                write(0, at, slab[k * per + s, 0, :, b * u : (b + 1) * u])
                    else:
                        for b in range(nf):
                            for s in range(per):
                                at = (slice(s * u, (s + 1) * u), slice(b * rows, (b + 1) * rows))
                                write(1, at, slab[3 * per + s, 0, :, b * u : (b + 1) * u].astype(F32).T)

    specs = [None] * 4
    for (matrix, _, count), start in zip(order, starts):
        specs[matrix] = pl.BlockSpec(
            (rows, have[matrix].shape[1] // count),
            lambda i, start=start, count=count: (0, jnp.clip(i - start, 0, count - 1)),
        )
    shapes = [jax.ShapeDtypeStruct(m.shape, F32) for m in have for _ in range(outs)]
    flat = pl.pallas_call(
        kernel,
        grid=(steps,),
        in_specs=[pl.BlockSpec(memory_space=pltpu.SMEM)] + [pl.BlockSpec(memory_space=pl.ANY)] * len(parts) + specs,
        out_specs=[spec for spec in specs for _ in range(outs)],
        out_shape=shapes,
        scratch_shapes=[
            pltpu.VMEM((nr, 3, rows, wide), BF),
            pltpu.SemaphoreType.DMA((len(parts), 3)),
        ],
        cost_estimate=pl.CostEstimate(
            flops=rows * rows * 100, transcendentals=0, bytes_accessed=(6 + 4 * outs) * sum(m.size for m in have)
        ),
    )(rep_scalar(), *parts, *have)
    return [tuple(flat[m * outs : (m + 1) * outs]) for m in range(4)]


def layer_norm_parts(values):
    center = values - jnp.mean(values, axis=-1, keepdims=True)
    spread = jnp.mean(center * center, axis=-1, keepdims=True)
    scale = lax.rsqrt(spread + 1e-05)
    return center * scale, scale


def gelu_tanh(values):
    return jax.nn.gelu(values, approximate=True)


def on_device(
    tokens,
    cotangent,
    qkv_weight,
    out_weight,
    up_weight,
    down_weight,
    ln_gain,
    ln_bias,
    up_bias,
    down_bias,
    qkv_moment,
    out_moment,
    up_moment,
    down_moment,
    gain_moment,
    beta_moment,
    up_bias_moment,
    down_bias_moment,
):
    nf = lax.axis_size("fsdp")
    nr = lax.axis_size("rep")
    f = lax.axis_index("fsdp")
    r = lax.axis_index("rep")
    _, local_len, width = tokens.shape
    rows = qkv_weight.shape[0]
    hidden_width = up_weight.shape[1] // nf
    head_width = width // nf
    unit = hidden_width // nr
    qkv_units = 3 * nr // 4

    tok = tokens.reshape(local_len, width)
    cot = cotangent.reshape(local_len, width)

    share = rows // nr
    core = rep_bit(0)
    spot = place(r, nr)
    is_out = spot >= qkv_units
    out_plane = is_out & (f == 1)

    def by_dest(weight, thirds):
        part = lax.dynamic_slice_in_dim(weight, r * share, share, 0)
        step = weight.shape[1] // thirds
        wide = step // nf
        return [
            jnp.concatenate([part[:, t * step + b * wide : t * step + (b + 1) * wide] for t in range(thirds)], axis=1)
            for b in range(nf)
        ]

    def slab_of(got):
        pieces = with_partner(plane_pieces(got, 0, nr), nr)
        return assemble(pieces, nr).reshape(width, got.shape[2])

    vectors = jnp.concatenate([ln_gain, ln_bias, down_bias]).reshape(1, 3 * rows)
    vectors = jnp.concatenate([vectors, jnp.zeros((7, 3 * rows), BF)], axis=0)
    got = z_exchange(jnp.stack([jnp.concatenate([w, vectors], axis=0) for w in by_dest(qkv_weight, 3)]))
    vectors = got[:, share].astype(F32)
    gain, beta, down_bias_full = [vectors[:, i * rows : (i + 1) * rows].reshape(width) for i in range(3)]
    qkv_cols = slab_of(got[:, :share])

    mlp = [jnp.concatenate(p, axis=1) for p in zip(by_dest(up_weight, 1), by_dest(down_weight, 1))]
    mlp = z_exchange(after(jnp.stack(mlp), got))
    mlp = slab_of(mlp)
    tok_near = z_neighbours(tok, nf)
    cot_near = z_neighbours(after(cot, *tok_near), nf)
    tok_all = z_gather(tok, tok_near, nf)
    length = tok_all.shape[0]
    cot_near = lax.optimization_barrier((*cot_near, tok_all))[:2]
    cot_all = z_gather(cot, cot_near, nf)
    up_cols, down_cols = mlp[:, :hidden_width], mlp[:, hidden_width:]

    xhat_all, _ = layer_norm_parts(tok_all.astype(F32))
    normed = (xhat_all * gain + beta).astype(BF)
    projected = jnp.dot(normed, qkv_cols, preferred_element_type=F32)
    tables = rotary_tables(length)
    q, k, v, probs, mixed = attend(projected, tables, head_width)
    hidden_pre = jnp.dot(normed, up_cols, preferred_element_type=F32) + up_bias.astype(F32)
    hidden_f, gelu_pull = jax.vjp(gelu_tanh, hidden_pre)
    hidden = hidden_f.astype(BF)

    def unit_columns(moment, thirds):
        step = moment.shape[1] // thirds
        wide = step // nf
        inside = jnp.minimum(spot, thirds * wide // unit - 1) * unit
        start = (inside // wide) * step + inside % wide
        parts = [lax.dynamic_slice_in_dim(moment, start + b * wide, unit, 1) for b in range(nf)]
        return jnp.concatenate(parts, axis=1)

    def side_by_side(blocks):
        return jnp.concatenate([blocks[b] for b in range(nf)], axis=1)

    held = lax.optimization_barrier((qkv_moment, out_moment, up_moment, down_moment, normed))[:4]
    out_start = jnp.maximum(spot - qkv_units, 0) * unit
    out_rows = lax.dynamic_slice_in_dim(held[1], out_start, unit, 0).T
    out_rows = side_by_side(out_rows.reshape(nf, rows, unit))
    owned = [unit_columns(held[0], 3), out_rows, unit_columns(held[2], 1), unit_columns(held[3], 1)]
    owned = [(MOMENTUM_RATE * m).astype(BF) for m in owned]
    owned = owned + [jnp.zeros((rows, nf * unit), BF)] * (nf - 4)
    moment_in = z_exchange(after(jnp.stack(owned), cot_all))
    moment_out = [side_by_side(moment_in[:, :, b * unit : (b + 1) * unit]) for b in range(nf)]
    moment_cols = jnp.where(out_plane, jnp.concatenate(moment_out, axis=0), moment_in.reshape(width, nf * unit))

    d_hidden = jnp.dot(cot_all, down_cols, preferred_element_type=F32)
    d_pre = gelu_pull(d_hidden)[0].astype(BF)
    lanes = nr // 2

    def joined(mine, other):
        return mine + xor_swap(other, 1, nr).astype(F32)

    order = high_bits(nr)
    mlp_parts = (d_pre, normed, hidden, cot_all, lanes)
    sum_mlp = joined(grad_mlp(core, *mlp_parts, F32), grad_mlp(1 - core, *mlp_parts, BF))
    unit_up, unit_down = plane_sum(sum_mlp[0], order, nr), plane_sum(sum_mlp[1], order[::-1], nr)

    d_mixed = contract(cot_all, out_weight, 1, 1).astype(BF)
    dq, dk, dv = attend_back(q, k, v, probs, d_mixed, tables)
    comb_parts = (dq, dk, dv, mixed, normed, cot_all, lanes)
    sum_comb = joined(grad_comb(core, *comb_parts, F32), grad_comb(1 - core, *comb_parts, BF))
    unit_comb = jnp.concatenate(
        [
            plane_sum(sum_comb[:, : unit // 2], order, nr),
            plane_sum(sum_comb[:, unit // 2 :], order[::-1], nr),
        ],
        axis=0,
    )

    partial_out = jnp.dot(mixed, out_weight, preferred_element_type=F32) + contract(hidden, down_cols, 1, 1)
    partial_out = partial_out.astype(BF).reshape(nf, local_len, width)
    summed = z_exchange(after(partial_out, moment_in))

    units = [u.astype(BF).T for u in (unit_comb, unit_up, unit_down)]
    sends = [units[0], units[0], units[1], units[2]] + [jnp.zeros((width, unit), BF)] * (nf - 4)
    grad_cols = z_exchange(after(jnp.stack(sends), summed))
    active = jnp.where(f == 0, ~is_out, jnp.where(f == 1, is_out, f < 4))
    s_cols = momentum_cols(active, moment_cols, grad_cols)

    s_pieces = plane_pieces(s_cols, 0, nr)
    gram = gram_of(s_pieces)
    gram_other = xor_swap(gram, 1, nr)

    grad_send = jnp.stack([jnp.stack([u[b * rows : (b + 1) * rows] for b in range(nf)]) for u in units], axis=1)
    grad_got = z_exchange(after(grad_send, grad_cols))
    kept = jnp.where(is_out, grad_send[:, 0], grad_got[:, 0])
    grad_mine = [side_by_side(g) for g in (kept, grad_got[:, 1], grad_got[:, 2])]
    grad_mine = after(jnp.stack(grad_mine), *[part for d in sorted(s_pieces) for part in s_pieces[d]])
    grad_pieces = {0: (grad_mine,)}
    for mask in range(2, nr, 2):
        grad_pieces[mask] = (xor_swap(grad_mine, mask, nr),)

    d_projected = jnp.concatenate([after(dq, grad_cols), dk, dv], axis=1)
    partial_normed = contract(d_projected, qkv_cols, 1, 1) + contract(d_pre, up_cols, 1, 1)
    partial_normed = partial_normed.astype(BF).reshape(nf, local_len, width)
    summed_normed = z_exchange(after(partial_normed, grad_got))

    ortho = orthogonalize(out_plane, gram, gram_other, s_cols, nf)
    back = z_exchange(after(ortho, summed_normed))
    ortho_mine = jnp.stack([jnp.where(is_out, back[1], back[0]), back[2], back[3]])
    ortho_pieces = with_partner(plane_pieces(ortho_mine, 1, nr), nr)

    mats = (qkv_weight, out_weight, up_weight, down_weight)
    moments = (qkv_moment, out_moment, up_moment, down_moment)
    done = finish(with_partner(grad_pieces, nr), moments, [grad_rule] * 4, 2, nr)
    grads, new_moments = [d[0] for d in done], [d[1] for d in done]
    rules = [weight_rule(MATRIX_RATE * 0.2 * math.sqrt(w.shape[1])) for w in mats]
    new_mats = [d[0] for d in finish(ortho_pieces, mats, rules, 1, nr)]

    inputs = tok.astype(F32)
    block_out = (inputs + jnp.sum(summed.astype(F32), axis=0) + down_bias_full).astype(BF)
    d_normed = jnp.sum(summed_normed.astype(F32), axis=0)
    xhat, inv_std = layer_norm_parts(inputs)
    e = d_normed * gain
    input_grad = cot.astype(F32) + inv_std * (
        e - jnp.mean(e, axis=-1, keepdims=True) - xhat * jnp.mean(e * xhat, axis=-1, keepdims=True)
    )

    pair = jnp.stack([jnp.sum(d_normed * xhat, axis=0), jnp.sum(d_normed, axis=0)])
    pair = pair.reshape(2, nf, rows).transpose(1, 0, 2)
    pair = jnp.sum(z_exchange(after(pair, back)), axis=0).reshape(2 * rows)
    down_sum = jnp.sum(lax.dynamic_slice_in_dim(cot_all, f * rows, rows, 1).astype(F32), axis=0)
    up_sum = jnp.sum(d_pre.astype(F32), axis=0)
    small = plane_sum_small(jnp.concatenate([pair, down_sum, up_sum]), nr)
    vec_grads = [small[:rows], small[rows : 2 * rows], small[3 * rows :], small[2 * rows : 3 * rows]]
    vec_moments = [
        MOMENTUM_RATE * m + g
        for m, g in zip((gain_moment, beta_moment, up_bias_moment, down_bias_moment), vec_grads)
    ]
    vec_new = [
        p.astype(F32) - VECTOR_RATE * m for p, m in zip((ln_gain, ln_bias, up_bias, down_bias), vec_moments)
    ]

    return (
        block_out.reshape(1, local_len, width),
        input_grad.reshape(1, local_len, width),
        *grads,
        *vec_grads,
        *new_mats,
        *vec_new,
        *new_moments,
        *vec_moments,
    )


def solution(mesh):
    split3 = P("rep", "fsdp", None)
    mat = P("fsdp", None)
    vec = P("fsdp")

    return jax.shard_map(
        on_device,
        mesh=mesh,
        in_specs=(split3,) * 2 + (mat,) * 4 + (vec,) * 4 + (mat,) * 4 + (vec,) * 4,
        out_specs=(split3,) * 2 + ((mat,) * 4 + (vec,) * 4) * 3,
        check_vma=False,
    )
```

```python
import math

import jax
import jax.numpy as jnp
from jax import lax
from jax.experimental import pallas as pl
from jax.experimental.pallas import tpu as pltpu
from jax.sharding import PartitionSpec as P


HEAD_DIM = 64
ROT = 32
NS = 5
QB = 256

MOMENTUM_RATE = 0.9
MATRIX_RATE = 0.05
VECTOR_RATE = 0.002
COEF_A = 3.4445
COEF_B = -4.775
COEF_C = 2.0315

BF = jnp.bfloat16
F32 = jnp.float32


def contract(left, right, left_dim, right_dim):
    return lax.dot_general(
        left, right, (((left_dim,), (right_dim,)), ((), ())), preferred_element_type=F32
    )


def after(x, *others):
    return lax.optimization_barrier((x,) + others)[0]


def z_neighbours(x, nf):
    right = lax.ppermute(x, "fsdp", [(i, i + 1) for i in range(nf - 1)])
    left = lax.ppermute(x, "fsdp", [(i, i - 1) for i in range(1, nf)])
    return right, left


def z_gather(x, near, nf):
    f = lax.axis_index("fsdp")
    length = x.shape[0]
    right, left = near
    from_left, from_right = [right], [left]
    for step in range(1, nf - 1):
        from_left.append(lax.ppermute(right, "fsdp", [(i, i + step) for i in range(1, nf - step)]))
        from_right.append(lax.ppermute(left, "fsdp", [(i, i - step) for i in range(step, nf - 1)]))
    line = jnp.concatenate(from_left[::-1] + [x] + from_right, axis=0)
    return lax.dynamic_slice_in_dim(line, (nf - 1 - f) * length, nf * length, 0)


def z_exchange(x):
    return lax.all_to_all(x, "fsdp", split_axis=0, concat_axis=0, tiled=True)


def xor_swap(x, mask, nr):
    return lax.ppermute(x, "rep", [(i, i ^ mask) for i in range(nr)])


def rep_bit(bit):
    return (lax.axis_index("rep") >> bit) & 1


def high_bits(nr):
    return list(range(1, nr.bit_length() - 1))


def place(index, nr):
    return (index & 1) * (nr // 2) + (index >> 1)


def plane_pieces(x, axis, nr):
    order = high_bits(nr)
    middle = x.shape[axis] // 2

    def halves(part):
        return lax.slice_in_dim(part, 0, middle, axis=axis), lax.slice_in_dim(part, middle, 2 * middle, axis=axis)

    if len(order) == 2:
        one, two = 1 << order[0], 1 << order[1]
        near, far = xor_swap(x, one, nr), xor_swap(x, two, nr)
        both = (xor_swap(halves(far)[0], one, nr), xor_swap(halves(near)[1], two, nr))
        return {0: (x,), one: (near,), two: (far,), one | two: both}
    sides = []
    for part, bits in zip(halves(x), (order[::-1], order)):
        held = {0: part}
        for bit in bits:
            for distance in list(held):
                held[distance | (1 << bit)] = xor_swap(held[distance], 1 << bit, nr)
        sides.append(held)
    return {distance: (sides[0][distance], sides[1][distance]) for distance in sides[0]}


def with_partner(pieces, nr):
    found = dict(pieces)
    for distance, parts in pieces.items():
        found[distance | 1] = tuple(xor_swap(part, 1, nr) for part in parts)
    return found


def listed(pieces):
    return [(d, n, len(pieces[d]), part) for d in sorted(pieces) for n, part in enumerate(pieces[d])]


def plane_sum_small(x, nr):
    for bit in range(nr.bit_length() - 1):
        x = x + xor_swap(x, 1 << bit, nr)
    return x


def rotary_tables(length):
    lane = jnp.arange(2 * HEAD_DIM, dtype=jnp.int32) % HEAD_DIM
    half = ROT // 2
    inverse = 10000.0 ** (-(2.0 * (lane % half).astype(F32)) / ROT)
    angles = jnp.arange(length, dtype=jnp.int32).astype(F32)[:, None] * inverse[None, :]
    cosine = jnp.where(lane < ROT, jnp.cos(angles), 1.0)
    sine = jnp.sin(angles)
    from_low = jnp.where((lane >= half) & (lane < ROT), sine, 0.0)
    from_high = jnp.where(lane < half, -sine, 0.0)
    return cosine, from_low, from_high


def turn(x, cosine, from_low, from_high):
    half = ROT // 2
    width = x.shape[1]
    return x * cosine + pltpu.roll(x, half, 1) * from_low + pltpu.roll(x, width - half, 1) * from_high


def attend_kernel(qf_ref, kf_ref, vf_ref, c_ref, lo_ref, hi_ref, q_ref, k_ref, v_ref, p_ref, o_ref):
    length = qf_ref.shape[0]
    cosine, low, high = c_ref[...], lo_ref[...], hi_ref[...]
    q_ref[...] = (turn(qf_ref[...], cosine, low, high).astype(BF).astype(F32) * HEAD_DIM ** (-0.5)).astype(BF)
    k_ref[...] = turn(kf_ref[...], cosine, low, high).astype(BF)
    v_ref[...] = vf_ref[...].astype(BF)
    row = lax.broadcasted_iota(jnp.int32, (QB, QB), 0)
    col = lax.broadcasted_iota(jnp.int32, (QB, QB), 1)
    for h in range(2):
        lanes = slice(h * HEAD_DIM, (h + 1) * HEAD_DIM)
        for i in range(length // QB):
            rows = slice(i * QB, (i + 1) * QB)
            seen = (i + 1) * QB
            s = contract(q_ref[rows, lanes], k_ref[:seen, lanes], 1, 1)
            last = jnp.where(row >= col, s[:, i * QB :], -1e30)
            s = last if i == 0 else jnp.concatenate([s[:, : i * QB], last], axis=1)
            e = jnp.exp(s - jnp.max(s, axis=1, keepdims=True))
            p = (e * (1.0 / jnp.sum(e, axis=1, keepdims=True))).astype(BF)
            p_ref[h, rows, :seen] = p
            o_ref[rows, lanes] = contract(p, v_ref[:seen, lanes], 1, 0).astype(BF)


def attend(projected, tables, width):
    length = projected.shape[0]
    pairs = width // (2 * HEAD_DIM)
    block = (length, 2 * HEAD_DIM)

    def at(third):
        return pl.BlockSpec(block, lambda h: (0, third * pairs + h))

    whole = pl.BlockSpec(block, lambda h: (0, 0))
    mine = pl.BlockSpec(block, lambda h: (0, h))
    piece = jax.ShapeDtypeStruct((length, width), BF)
    return pl.pallas_call(
        attend_kernel,
        grid=(pairs,),
        in_specs=[at(0), at(1), at(2), whole, whole, whole],
        out_specs=[mine, mine, mine, pl.BlockSpec((2, length, length), lambda h: (h, 0, 0)), mine],
        out_shape=[piece, piece, piece, jax.ShapeDtypeStruct((2 * pairs, length, length), BF), piece],
        name="attend",
    )(projected, projected, projected, *tables)


def attend_back(core, q, k, v, probs, cot, out_weight, mixed, normed, tables, unit):
    length, width = q.shape
    lanes = 2 * HEAD_DIM
    pairs = width // lanes
    model = cot.shape[1]
    blocks = length // QB
    group = lanes // unit
    half_rot = ROT // 2

    def kernel(
        w_ref, q_ref, k_ref, v_ref, p_ref, y_ref, o_ref, m_ref, x_ref, c_ref, lo_ref, hi_ref,
        d_ref, other_ref, own_ref, do_ref, turned, ds_ref, acc
    ):
        do = contract(y_ref[...], o_ref[...], 1, 1).astype(BF)
        do_ref[...] = do
        for n, x in enumerate((q_ref[...], k_ref[...], do)):
            turned[n] = x.T
        for h in range(2):
            at = slice(h * HEAD_DIM, (h + 1) * HEAD_DIM)
            for i in range(blocks):
                rows = slice(i * QB, (i + 1) * QB)
                seen = (i + 1) * QB
                p = p_ref[h, rows, :seen].astype(F32)
                dp = contract(do_ref[rows, at], v_ref[:seen, at], 1, 1)
                ds = (p * (dp - jnp.sum(p * dp, axis=1, keepdims=True))).astype(BF)
                ds_ref[rows, :seen] = ds
                acc[0, at, rows] = contract(turned[1, at, :seen], ds, 1, 1) * HEAD_DIM ** (-0.5)
            for j in range(blocks):
                cols = slice(j * QB, (j + 1) * QB)
                rest = slice(j * QB, length)
                acc[1, at, cols] = contract(turned[0, at, rest], ds_ref[rest, cols], 1, 0)
                acc[2, at, cols] = contract(turned[2, at, rest], p_ref[h, rest, cols], 1, 0)
        cosine, low, high = c_ref[...], lo_ref[...], hi_ref[...]
        for n in range(2):
            x = acc[n]
            x = x * cosine - pltpu.roll(x, half_rot, 0) * low - pltpu.roll(x, lanes - half_rot, 0) * high
            d_ref[n] = x.astype(BF)
        d_ref[2] = acc[2].astype(BF)
        for n in range(4):
            left = m_ref[...].T if n == 3 else d_ref[n]
            grad = contract(left, y_ref[...] if n == 3 else x_ref[...], 1, 0).reshape(group, unit, model)

            @pl.when(w_ref[0] == n // 2)
            def _(n=n, grad=grad):
                own_ref[n % 2, 0] = grad

            @pl.when(w_ref[0] != n // 2)
            def _(n=n, grad=grad):
                other_ref[n % 2, 0] = grad.astype(BF)

    block = (length, lanes)
    mine = pl.BlockSpec(block, lambda h, w: (0, h))
    table = pl.BlockSpec(block[::-1], lambda h, w: (0, 0))
    whole = pl.BlockSpec((length, model), lambda h, w: (0, 0))
    grads = pl.BlockSpec((2, 1, group, unit, model), lambda h, w: (0, h, 0, 0, 0))
    shape = (2, pairs, group, unit, model)
    d_all, other, own = pl.pallas_call(
        kernel,
        grid_spec=pltpu.PrefetchScalarGridSpec(
            num_scalar_prefetch=1,
            grid=(pairs,),
            in_specs=[
                mine,
                mine,
                mine,
                pl.BlockSpec((2, length, length), lambda h, w: (h, 0, 0)),
                whole,
                pl.BlockSpec((lanes, model), lambda h, w: (h, 0)),
                mine,
                whole,
                table,
                table,
                table,
            ],
            out_specs=[pl.BlockSpec((3, lanes, length), lambda h, w: (0, h, 0)), grads, grads],
            scratch_shapes=[
                pltpu.VMEM(block, BF),
                pltpu.VMEM((3,) + block[::-1], BF),
                pltpu.VMEM((length, length), BF),
                pltpu.VMEM((3,) + block[::-1], F32),
            ],
        ),
        out_shape=[
            jax.ShapeDtypeStruct((3, width, length), BF),
            jax.ShapeDtypeStruct(shape, BF),
            jax.ShapeDtypeStruct(shape, F32),
        ],
        cost_estimate=pl.CostEstimate(
            flops=24 * length * length * width, transcendentals=0, bytes_accessed=8 * length * length
        ),
        name="attend_back",
    )(core.astype(jnp.int32).reshape(1), q, k, v, probs, cot, out_weight, mixed, normed, *[t.T for t in tables])
    flat = (2 * pairs * group, unit, model)
    return d_all.reshape(3 * width, length), other.reshape(flat), own.reshape(flat)


def split(x):
    high = x.astype(BF)
    return high, (x - high.astype(F32)).astype(BF)


def upper(count):
    return [(i, j) for i in range(count) for j in range(i, count)]


def gram_of(pieces):
    entries = listed(pieces)
    slots = sorted(pieces)
    size = sum(part.shape[0] for part in pieces[0])
    wide = pieces[0][0].shape[1]
    count = size // QB

    def kernel(*refs):
        ins, out, slab, sems = refs[:-3], refs[-3], refs[-2], refs[-1]
        copies = []
        for k, (d, n, _, part) in enumerate(entries):
            rows = part.shape[0]
            to = slab.at[pl.ds(n * rows, rows), pl.ds(slots.index(d) * wide, wide)]
            copies.append(pltpu.make_async_copy(ins[k], to, sems.at[k]))
        for copy in copies:
            copy.start()
        for copy in copies:
            copy.wait()
        for i in range(count):
            strip = contract(slab[i * QB : (i + 1) * QB], slab[i * QB :], 1, 1)
            for j in range(i, count):
                out[upper(count).index((i, j))] = strip[:, (j - i) * QB : (j - i + 1) * QB]

    return pl.pallas_call(
        kernel,
        in_specs=[pl.BlockSpec(memory_space=pl.ANY)] * len(entries),
        out_specs=pl.BlockSpec(memory_space=pltpu.VMEM),
        out_shape=jax.ShapeDtypeStruct((count * (count + 1) // 2, QB, QB), F32),
        scratch_shapes=[
            pltpu.VMEM((size, wide * len(slots)), BF),
            pltpu.SemaphoreType.DMA((len(entries),)),
        ],
        cost_estimate=pl.CostEstimate(
            flops=2 * size * size * wide * len(slots), transcendentals=0, bytes_accessed=2 * size * wide * len(slots)
        ),
        name="gram",
    )(*[part for _, _, _, part in entries])


def ortho_kernel(flag_ref, ga_ref, gb_ref, s_ref, out_ref, x_ref, gh, gl, th, tl, pm):
    size = gh.shape[0]
    count = size // QB
    parts = [slice(i * QB, (i + 1) * QB) for i in range(count)]
    pairs = upper(count)
    trace = jnp.zeros((), F32)
    row = lax.broadcasted_iota(jnp.int32, (QB, QB), 0)
    col = lax.broadcasted_iota(jnp.int32, (QB, QB), 1)
    for i in range(count):
        n = pairs.index((i, i))
        trace = trace + jnp.sum(jnp.where(row == col, ga_ref[n] + gb_ref[n], 0.0))
    scale = 1.0 / (jnp.sqrt(jnp.broadcast_to(trace, (1, 1))) + 1e-07)

    def put(i, j, block):
        high, low = split(block)
        gh[parts[i], parts[j]], gl[parts[i], parts[j]] = high, low
        if i != j:
            turned = block.T
            high, low = split(turned)
            gh[parts[j], parts[i]], gl[parts[j], parts[i]] = high, low

    for n, (i, j) in enumerate(pairs):
        put(i, j, (ga_ref[n] + gb_ref[n]) * (scale * scale))
    x_ref[...] = (s_ref[...].astype(F32) * scale).astype(BF)

    def poly():
        for i in range(count):
            rest = slice(i * QB, size)
            square = contract(gh[parts[i]], gh[:, rest], 1, 0)
            block = COEF_B * gh[parts[i], rest].astype(F32) + COEF_C * square
            pm[parts[i], rest] = block.astype(BF)
            for j in range(i + 1, count):
                pm[parts[j], parts[i]] = block[:, (j - i) * QB : (j - i + 1) * QB].T.astype(BF)

    def advance():
        x = x_ref[...]
        x_ref[...] = (COEF_A * x.astype(F32) + contract(pm[...], x, 1, 0)).astype(BF)

    def body(_, carry):
        poly()
        advance()
        for part in parts:
            left = pm[part]
            total = COEF_A * (gh[part].astype(F32) + gl[part].astype(F32))
            total = total + contract(left, gh[...], 1, 0) + contract(left, gl[...], 1, 0)
            th[part], tl[part] = split(total)
        for i in range(count):
            rest = slice(i * QB, size)
            total = COEF_A * (th[parts[i], rest].astype(F32) + tl[parts[i], rest].astype(F32))
            total = total + contract(th[parts[i]], pm[:, rest], 1, 0) + contract(tl[parts[i]], pm[:, rest], 1, 0)
            for j in range(i, count):
                put(i, j, total[:, (j - i) * QB : (j - i + 1) * QB])
        return carry

    lax.fori_loop(0, NS - 1, body, 0)
    poly()
    advance()
    nf, wide, _ = out_ref.shape
    unit = x_ref.shape[1] // nf

    @pl.when(flag_ref[0] == 0)
    def _():
        for a in range(nf):
            out_ref[a] = x_ref[a * wide : (a + 1) * wide]

    @pl.when(flag_ref[0] == 1)
    def _():
        for a in range(nf):
            for b in range(nf):
                out_ref[b, :, a * unit : (a + 1) * unit] = x_ref[a * wide : (a + 1) * wide, b * unit : (b + 1) * unit]


def orthogonalize(swapped, gram_a, gram_b, cols, nf):
    size = cols.shape[0]
    square = pltpu.VMEM((size, size), BF)
    vmem = pl.BlockSpec(memory_space=pltpu.VMEM)
    return pl.pallas_call(
        ortho_kernel,
        in_specs=[pl.BlockSpec(memory_space=pltpu.SMEM), vmem, vmem, vmem],
        out_specs=vmem,
        out_shape=jax.ShapeDtypeStruct((nf, size // nf, cols.shape[1]), BF),
        scratch_shapes=[pltpu.VMEM(cols.shape, BF)] + [square] * 5,
        cost_estimate=pl.CostEstimate(
            flops=40 * size**3, transcendentals=0, bytes_accessed=8 * size * size
        ),
        name="orthogonalize",
    )(swapped.astype(jnp.int32).reshape(1), gram_a, gram_b, cols)


def momentum_cols(mode, moment, grads):
    nf, size, unit = grads.shape
    rows = size // nf

    def kernel(mode_ref, m_ref, g_ref, out_ref):
        def fill(pick):
            for a in range(nf):
                for b in range(nf):
                    at = (slice(a * rows, (a + 1) * rows), slice(b * unit, (b + 1) * unit))
                    out_ref[at] = pick(a, b)

        def block(a, b):
            return m_ref[a, :, b * unit : (b + 1) * unit].astype(F32)

        def grad(a, b):
            return g_ref[b, a * rows : (a + 1) * rows].astype(F32)

        @pl.when(mode_ref[0] == 0)
        def _():
            out_ref[...] = jnp.zeros(out_ref.shape, BF)

        @pl.when(mode_ref[0] == 1)
        def _():
            fill(lambda a, b: (block(a, b) + grad(a, b)).astype(BF))

        @pl.when(mode_ref[0] == 2)
        def _():
            fill(lambda a, b: (block(b, a) + grad(a, b)).astype(BF))

    vmem = pl.BlockSpec(memory_space=pltpu.VMEM)
    return pl.pallas_call(
        kernel,
        in_specs=[pl.BlockSpec(memory_space=pltpu.SMEM), vmem, vmem],
        out_specs=vmem,
        out_shape=jax.ShapeDtypeStruct((size, nf * unit), BF),
        name="momentum_cols",
    )(mode.astype(jnp.int32).reshape(1), moment, grads)


def rep_scalar():
    return lax.axis_index("rep").astype(jnp.int32).reshape(1)


def assemble(pieces, nr):
    entries = listed(pieces)
    count = sum(part.shape[0] for part in pieces[0])
    tail = pieces[0][0].shape[1:]

    def kernel(r_ref, *refs):
        ins, out, sems = refs[:-2], refs[-2], refs[-1]
        copies = []
        for k, (d, n, _, part) in enumerate(entries):
            to = out.at[pl.ds(n * part.shape[0], part.shape[0]), r_ref[0] ^ d]
            copies.append(pltpu.make_async_copy(ins[k], to, sems.at[k]))
        for copy in copies:
            copy.start()
        for copy in copies:
            copy.wait()

    return pl.pallas_call(
        kernel,
        in_specs=[pl.BlockSpec(memory_space=pltpu.SMEM)] + [pl.BlockSpec(memory_space=pl.ANY)] * len(entries),
        out_specs=pl.BlockSpec(memory_space=pltpu.VMEM),
        out_shape=jax.ShapeDtypeStruct((count, nr) + tail, pieces[0][0].dtype),
        scratch_shapes=[pltpu.SemaphoreType.DMA((len(entries),))],
    )(rep_scalar(), *[part for _, _, _, part in entries])


def feed_forward(core, normed, cot, slab, bias, lanes):
    length, width = normed.shape
    total = slab.shape[1] // 2
    mid = total // 2
    step = min(mid, QB)
    count = mid // step
    unit = mid // lanes
    group = step // unit
    root = (2.0 / 3.141592653589793) ** 0.5

    def kernel(w_ref, x_ref, y_ref, up_ref, down_ref, b_ref, h_ref, d_ref, sum_ref, other_ref, gu_ref, gd_ref):
        x, y = x_ref[...], y_ref[...]
        v = contract(x, up_ref[...], 1, 0) + b_ref[...]
        t = jnp.tanh(root * (v + 0.044715 * (v * v * v)))
        hidden = (0.5 * v * (1.0 + t)).astype(BF)
        slope = 0.5 * (1.0 + t) + 0.5 * v * (1.0 - t * t) * (root * (1.0 + 3 * 0.044715 * (v * v)))
        d_pre = (contract(y, down_ref[...], 1, 0) * slope).astype(BF)
        h_ref[...] = hidden
        d_ref[...] = d_pre
        sum_ref[...] = jnp.sum(d_pre.astype(F32), axis=0, keepdims=True)
        up = contract(d_pre, x, 0, 0).reshape(group, unit, width)
        down = contract(hidden, y, 0, 0).reshape(group, unit, width)

        @pl.when(pl.program_id(0) < count)
        def _():
            other_ref[0] = up.astype(BF)
            other_ref[1] = down.astype(BF)

        @pl.when(pl.program_id(0) >= count)
        def _():
            gu_ref[...] = up
            gd_ref[...] = down

    def at(i, w):
        return jnp.where(i < count, (1 - w[0]) * count + i, w[0] * count + i - count)

    whole = pl.BlockSpec((length, width), lambda i, w: (0, 0))
    tall = pl.BlockSpec((length, step), lambda i, w: (0, at(i, w)))
    own = pl.BlockSpec((group, unit, width), lambda i, w: (jnp.maximum(i - count, 0), 0, 0))
    return pl.pallas_call(
        kernel,
        grid_spec=pltpu.PrefetchScalarGridSpec(
            num_scalar_prefetch=1,
            grid=(2 * count,),
            in_specs=[
                whole,
                whole,
                pl.BlockSpec((width, step), lambda i, w: (0, at(i, w))),
                pl.BlockSpec((width, step), lambda i, w: (0, 2 * count + at(i, w))),
                pl.BlockSpec((1, step), lambda i, w: (0, at(i, w))),
            ],
            out_specs=[
                tall,
                tall,
                pl.BlockSpec((1, step), lambda i, w: (0, at(i, w))),
                pl.BlockSpec((2, group, unit, width), lambda i, w: (0, jnp.minimum(i, count - 1), 0, 0)),
                own,
                own,
            ],
        ),
        out_shape=[
            jax.ShapeDtypeStruct((length, total), BF),
            jax.ShapeDtypeStruct((length, total), BF),
            jax.ShapeDtypeStruct((1, total), F32),
            jax.ShapeDtypeStruct((2, lanes, unit, width), BF),
            jax.ShapeDtypeStruct((lanes, unit, width), F32),
            jax.ShapeDtypeStruct((lanes, unit, width), F32),
        ],
        cost_estimate=pl.CostEstimate(
            flops=8 * length * width * total, transcendentals=length * total, bytes_accessed=20 * length * width
        ),
        name="feed_forward",
    )(core.astype(jnp.int32).reshape(1), normed, cot, slab, slab, bias)


def fold(items):
    shapes, arrays = [], []
    for own, (got, _), cut, _, _ in items:
        rows = cut.stop - cut.start
        shapes += [
            jax.ShapeDtypeStruct((own.shape[0] // 2, rows, own.shape[2]), BF),
            jax.ShapeDtypeStruct((own.shape[0] // 2, rows, own.shape[2]), F32),
        ]
        arrays += [own, got]
    count = len(items)

    def kernel(r_ref, *refs):
        ins, outs = refs[: 2 * count], refs[2 * count :]
        for k, (own, (_, index), cut, held, bit) in enumerate(items):
            low = sum(1 for b in held if b < bit)
            value = (r_ref[0] >> bit) & 1
            for n in range(own.shape[0] // 2):
                base = ((n >> low) << (low + 1)) | (n & ((1 << low) - 1))

                def total(choice, k=k, base=base, low=low, cut=cut, index=index):
                    at = base | (choice << low)
                    got = ins[2 * k + 1][at, cut] if index is None else ins[2 * k + 1][index, at, cut]
                    return ins[2 * k][at, cut] + got.astype(F32)

                outs[2 * k][n] = total(1 - value).astype(BF)
                outs[2 * k + 1][n] = total(value)

    vmem = pl.BlockSpec(memory_space=pltpu.VMEM)
    flat = pl.pallas_call(
        kernel,
        in_specs=[pl.BlockSpec(memory_space=pltpu.SMEM)] + [vmem] * (2 * count),
        out_specs=[vmem] * (2 * count),
        out_shape=shapes,
    )(rep_scalar(), *arrays)
    return [(flat[2 * k], flat[2 * k + 1]) for k in range(count)]


def units_kernel(parts, nf):
    flat = [x for part in parts for pair in part for x in pair]
    unit = sum(x.shape[0] for x, _ in parts[0])
    width = flat[0].shape[1]
    rows = width // nf

    def kernel(*refs):
        ins, plane_ref, row_ref = refs[:-2], refs[-2], refs[-1]
        n = 0
        for m, part in enumerate(parts):
            blocks = []
            for _ in part:
                blocks.append(ins[n][...] + ins[n + 1][...].astype(F32))
                n += 2
            block = (blocks[0] if len(blocks) == 1 else jnp.concatenate(blocks, axis=0)).T.astype(BF)
            for to in ((0, 1), (2,), (3,))[m]:
                plane_ref[to] = block
            for b in range(nf):
                row_ref[b, m] = block[b * rows : (b + 1) * rows]
        for to in range(4, nf):
            plane_ref[to] = jnp.zeros((width, unit), BF)

    vmem = pl.BlockSpec(memory_space=pltpu.VMEM)
    return pl.pallas_call(
        kernel,
        in_specs=[vmem] * len(flat),
        out_specs=[vmem] * 2,
        out_shape=[
            jax.ShapeDtypeStruct((nf, width, unit), BF),
            jax.ShapeDtypeStruct((nf, 3, rows, unit), BF),
        ],
        name="units",
    )(*flat)


def moment_units(spot, qkv, out, up, down, nf, nr):
    rows, width = out.shape
    unit = up.shape[1] // (nf * nr)
    per = nr // 4
    units = 3 * per

    def kernel(s_ref, q_ref, o_ref, u_ref, d_ref, out_ref):
        for n, block in enumerate((q_ref[...], o_ref[...].T, u_ref[...], d_ref[...])):
            out_ref[n] = (MOMENTUM_RATE * block).astype(BF)
        for n in range(4, nf):
            out_ref[n] = jnp.zeros((rows, unit), BF)

    def qkv_at(b, s):
        inside = jnp.minimum(s[0], units - 1)
        return (0, (inside // per) * (width // unit) + b * per + inside % per)

    return pl.pallas_call(
        kernel,
        grid_spec=pltpu.PrefetchScalarGridSpec(
            num_scalar_prefetch=1,
            grid=(nf,),
            in_specs=[
                pl.BlockSpec((rows, unit), qkv_at),
                pl.BlockSpec((unit, rows), lambda b, s: (jnp.maximum(s[0] - units, 0), b)),
                pl.BlockSpec((rows, unit), lambda b, s: (0, b * nr + s[0])),
                pl.BlockSpec((rows, unit), lambda b, s: (0, b * nr + s[0])),
            ],
            out_specs=pl.BlockSpec((nf, rows, unit), lambda b, s: (0, 0, b)),
        ),
        out_shape=jax.ShapeDtypeStruct((nf, rows, nf * unit), BF),
        name="moment_units",
    )(spot.astype(jnp.int32).reshape(1), qkv, out, up, down)


def grad_rule(block, have):
    return block, MOMENTUM_RATE * have + block


def weight_rule(step):
    def rule(block, have):
        return (have.astype(F32) - step * block,)

    return rule


def finish_plain(pieces, have, rules, nr, subset):
    whole = jnp.stack([jnp.concatenate(pieces[d], axis=1) for d in sorted(pieces)])
    index = jnp.arange(nr)
    source = (index // (nr // 2)) | ((index % (nr // 2)) << 1)
    whole = whole[source ^ lax.axis_index("rep")]
    per = nr // 4
    rows = whole.shape[2]
    nf = have[1].shape[1] // rows
    whole = whole.reshape(nr, 3, rows, nf, -1)
    unit = whole.shape[4]
    qkv = whole[: 3 * per, 0].reshape(3, per, rows, nf, unit).transpose(2, 0, 3, 1, 4).reshape(rows, -1)
    out = whole[3 * per :, 0].transpose(0, 3, 2, 1).reshape(rows, -1)
    up = whole[:, 1].transpose(1, 2, 0, 3).reshape(rows, -1)
    down = whole[:, 2].transpose(1, 2, 0, 3).reshape(rows, -1)
    whole = (qkv, out, up, down)
    return [rules[m](whole[m].astype(F32), have[m]) for m in subset]


def finish(pieces, have, rules, outs, nr, subset):
    entries = listed(pieces)
    parts = [part for _, _, _, part in entries]
    wide = parts[0].shape[2]
    rows = sum(part.shape[1] for part in pieces[0])
    nf = have[1].shape[1] // rows
    u = wide // nf
    if u % 128:
        return finish_plain(pieces, have, rules, nr, subset)
    per = nr // 4
    order = [x for x in ((2, 1, nf), (3, 2, nf), (0, 0, 3), (1, 0, 1)) if x[0] in subset]
    starts = [sum(x[2] for x in order[:n]) for n in range(len(order))]
    steps = sum(x[2] for x in order)
    spot = {matrix: n for n, matrix in enumerate(subset)}
    many = len(subset)

    def kernel(r_ref, *refs):
        ins = refs[: len(parts)]
        have_refs = refs[len(parts) : len(parts) + many]
        out_refs = refs[len(parts) + many : len(parts) + many + many * outs]
        slab, sems = refs[-2:]
        step = pl.program_id(0)

        def copies(which):
            for k, (d, n, _, part) in enumerate(entries):
                to = slab.at[place(r_ref[0] ^ d, nr), which, pl.ds(n * part.shape[1], part.shape[1])]
                yield pltpu.make_async_copy(ins[k].at[which], to, sems.at[k, which])

        @pl.when(step == 0)
        def _():
            for which in dict.fromkeys(x[1] for x in order):
                for copy in copies(which):
                    copy.start()

        def write(matrix, at, block):
            values = rules[matrix](block.astype(F32), have_refs[spot[matrix]][at])
            for n, value in enumerate(values):
                out_refs[spot[matrix] * outs + n][at] = value

        for (matrix, which, count), start in zip(order, starts):
            for k in range(count):

                @pl.when(step == start + k)
                def _(matrix=matrix, which=which, start=start, k=k):
                    if k == 0 and matrix != 1:
                        for copy in copies(which):
                            copy.wait()
                    if matrix >= 2:
                        for p in range(nr):
                            at = (slice(None), slice(p * u, (p + 1) * u))
                            write(matrix, at, slab[p, which, :, k * u : (k + 1) * u])
                    elif matrix == 0:
                        for b in range(nf):
                            for s in range(per):
                                at = (slice(None), slice((b * per + s) * u, (b * per + s + 1) * u))
                                write(0, at, slab[k * per + s, 0, :, b * u : (b + 1) * u])
                    else:
                        for b in range(nf):
                            for s in range(per):
                                at = (slice(s * u, (s + 1) * u), slice(b * rows, (b + 1) * rows))
                                write(1, at, slab[3 * per + s, 0, :, b * u : (b + 1) * u].astype(F32).T)

    specs = [None] * many
    for (matrix, _, count), start in zip(order, starts):
        specs[spot[matrix]] = pl.BlockSpec(
            (rows, have[matrix].shape[1] // count),
            lambda i, start=start, count=count: (0, jnp.clip(i - start, 0, count - 1)),
        )
    taken = [have[m] for m in subset]
    shapes = [jax.ShapeDtypeStruct(m.shape, F32) for m in taken for _ in range(outs)]
    flat = pl.pallas_call(
        kernel,
        grid=(steps,),
        in_specs=[pl.BlockSpec(memory_space=pltpu.SMEM)] + [pl.BlockSpec(memory_space=pl.ANY)] * len(parts) + specs,
        out_specs=[spec for spec in specs for _ in range(outs)],
        out_shape=shapes,
        scratch_shapes=[
            pltpu.VMEM((nr, 3, rows, wide), BF),
            pltpu.SemaphoreType.DMA((len(parts), 3)),
        ],
        cost_estimate=pl.CostEstimate(
            flops=rows * rows * 100, transcendentals=0, bytes_accessed=(6 + 4 * outs) * sum(m.size for m in taken)
        ),
    )(rep_scalar(), *parts, *taken)
    return [tuple(flat[m * outs : (m + 1) * outs]) for m in range(many)]


def layer_norm_parts(values):
    center = values - jnp.mean(values, axis=-1, keepdims=True)
    spread = jnp.mean(center * center, axis=-1, keepdims=True)
    scale = lax.rsqrt(spread + 1e-05)
    return center * scale, scale


def on_device(
    tokens,
    cotangent,
    qkv_weight,
    out_weight,
    up_weight,
    down_weight,
    ln_gain,
    ln_bias,
    up_bias,
    down_bias,
    qkv_moment,
    out_moment,
    up_moment,
    down_moment,
    gain_moment,
    beta_moment,
    up_bias_moment,
    down_bias_moment,
):
    nf = lax.axis_size("fsdp")
    nr = lax.axis_size("rep")
    f = lax.axis_index("fsdp")
    r = lax.axis_index("rep")
    _, local_len, width = tokens.shape
    rows = qkv_weight.shape[0]
    hidden_width = up_weight.shape[1] // nf
    head_width = width // nf
    unit = hidden_width // nr
    qkv_units = 3 * nr // 4

    tok = tokens.reshape(local_len, width)
    cot = cotangent.reshape(local_len, width)

    share = rows // nr
    core = rep_bit(0)
    spot = place(r, nr)
    is_out = spot >= qkv_units
    out_plane = is_out & (f == 1)

    def by_dest(weight, thirds):
        part = lax.dynamic_slice_in_dim(weight, r * share, share, 0)
        step = weight.shape[1] // thirds
        wide = step // nf
        return [
            jnp.concatenate([part[:, t * step + b * wide : t * step + (b + 1) * wide] for t in range(thirds)], axis=1)
            for b in range(nf)
        ]

    def slab_of(got):
        pieces = with_partner(plane_pieces(got, 0, nr), nr)
        return assemble(pieces, nr).reshape(width, got.shape[2])

    vectors = jnp.concatenate([ln_gain, ln_bias, down_bias]).reshape(1, 3 * rows)
    vectors = jnp.concatenate([vectors, jnp.zeros((7, 3 * rows), BF)], axis=0)
    got = z_exchange(jnp.stack([jnp.concatenate([w, vectors], axis=0) for w in by_dest(qkv_weight, 3)]))
    vectors = got[:, share].astype(F32)
    gain, beta, down_bias_full = [vectors[:, i * rows : (i + 1) * rows].reshape(width) for i in range(3)]
    qkv_cols = slab_of(got[:, :share])

    mlp = [jnp.concatenate(p, axis=1) for p in zip(by_dest(up_weight, 1), by_dest(down_weight, 1))]
    mlp = z_exchange(after(jnp.stack(mlp), got))
    mlp_pieces = plane_pieces(mlp, 0, nr)
    tok_near = z_neighbours(tok, nf)
    cot_near = z_neighbours(after(cot, *tok_near), nf)
    tok_all = z_gather(tok, tok_near, nf)
    length = tok_all.shape[0]

    xhat_all, _ = layer_norm_parts(tok_all.astype(F32))
    normed = (xhat_all * gain + beta).astype(BF)
    projected = jnp.dot(normed, qkv_cols, preferred_element_type=F32)

    def side_by_side(blocks):
        return jnp.concatenate([blocks[b] for b in range(nf)], axis=1)

    def unit_columns(moment, thirds):
        step = moment.shape[1] // thirds
        wide = step // nf
        inside = jnp.minimum(spot, thirds * wide // unit - 1) * unit
        start = (inside // wide) * step + inside % wide
        return jnp.concatenate([lax.dynamic_slice_in_dim(moment, start + b * wide, unit, 1) for b in range(nf)], axis=1)

    held = lax.optimization_barrier((qkv_moment, out_moment, up_moment, down_moment, got))[:4]
    if unit % 128:
        out_start = jnp.maximum(spot - qkv_units, 0) * unit
        out_rows = lax.dynamic_slice_in_dim(held[1], out_start, unit, 0).T
        out_rows = side_by_side(out_rows.reshape(nf, rows, unit))
        owned = [unit_columns(held[0], 3), out_rows, unit_columns(held[2], 1), unit_columns(held[3], 1)]
        owned = [(MOMENTUM_RATE * m).astype(BF) for m in owned]
        owned = jnp.stack(owned + [jnp.zeros((rows, nf * unit), BF)] * (nf - 4))
    else:
        owned = moment_units(spot, *held, nf, nr)
    cot_near = lax.optimization_barrier((*cot_near, projected))[:2]
    cot_all = z_gather(cot, cot_near, nf)
    tables = rotary_tables(length)
    q, k, v, probs, mixed = attend(projected, tables, head_width)
    mlp_pieces = with_partner(mlp_pieces, nr)
    mlp = assemble(mlp_pieces, nr).reshape(width, 2 * hidden_width)
    up_cols, down_cols = mlp[:, :hidden_width], mlp[:, hidden_width:]
    moment_in = z_exchange(after(owned, cot_all))

    lanes = nr // 2
    order = high_bits(nr)
    every = slice(0, unit)
    hidden, d_pre, up_sum, other, grad_up, grad_down = feed_forward(
        core, normed, cot_all, after(mlp, mixed), up_bias.astype(F32).reshape(1, hidden_width), lanes
    )
    other = xor_swap(other, 1, nr)

    def send(results, bits):
        return [(own, (xor_swap(away, 1 << bit, nr), None)) for (away, own), bit in zip(results, bits)]

    ways = (order, order[::-1])
    state = [(grad_up, (other, 0)), (grad_down, (other, 1))]
    steps = []
    for n in range(len(order)):
        bits = [way[n] for way in ways]
        left = [[b for b in order if b not in way[:n]] for way in ways]
        done = fold([(*x, every, h, b) for x, h, b in zip(state, left, bits)])
        steps.append(done)
        state = send(done, bits)
        if n == 0:
            q = after(q, *[x for pair in done for x in pair])
            d_projected, other, grad_own = attend_back(
                core, q, k, v, probs, cot_all, out_weight, mixed, normed, tables, unit
            )
    mlp_state = state
    other = xor_swap(after(other, *[x for pair in steps[-1] for x in pair]), 1, nr)
    state = [(grad_own, (other, None))] * 2
    cuts = (slice(0, unit // 2), slice(unit // 2, unit))
    for n in range(len(order)):
        bits = [way[n] for way in ways]
        left = [[b for b in order if b not in way[:n]] for way in ways]
        if n:
            cuts = (slice(0, unit // 2),) * 2
        done = fold([(*x, c, h, b) for x, c, h, b in zip(state, cuts, left, bits)])
        state = send(done, bits)
    plane_send, grad_send = units_kernel(
        [[(own[0], got[0]) for own, (got, _) in part] for part in (state, mlp_state[:1], mlp_state[1:])], nf
    )

    cut = 5 * local_len // 8
    mixed, hidden = lax.optimization_barrier((mixed, hidden, grad_own))[:2]
    partial_out = jnp.dot(mixed, out_weight, preferred_element_type=F32) + contract(hidden, down_cols, 1, 1)
    partial_out = partial_out.astype(BF).reshape(nf, local_len, width)
    summed = z_exchange(after(partial_out[:, :cut], moment_in))

    grad_cols = z_exchange(after(plane_send, summed))
    mode = jnp.where(f == 0, ~is_out, jnp.where(f == 1, 2 * is_out, f < 4))
    s_cols = momentum_cols(mode, moment_in, grad_cols)

    s_pieces = plane_pieces(s_cols, 0, nr)

    grad_got = z_exchange(after(grad_send, grad_cols))
    kept = jnp.where(is_out, grad_send[:, 0], grad_got[:, 0])
    grad_mine = [side_by_side(g) for g in (kept, grad_got[:, 1], grad_got[:, 2])]
    grad_mine = after(jnp.stack(grad_mine), *[part for d in sorted(s_pieces) for part in s_pieces[d]])
    grad_pieces = {0: (grad_mine,)}
    for mask in range(2, nr, 2):
        grad_pieces[mask] = (xor_swap(grad_mine, mask, nr),)

    d_projected = after(d_projected, grad_cols)
    partial_normed = contract(d_projected, qkv_cols, 0, 1) + contract(d_pre, up_cols, 1, 1)
    pair = jnp.stack([jnp.sum(partial_normed * xhat_all, axis=0), jnp.sum(partial_normed, axis=0)])
    pair = pair.reshape(2, nf, rows).transpose(1, 0, 2)
    pair = jnp.pad(pair, ((0, 0), (0, 6), (0, width - rows))).astype(BF)
    partial_normed = partial_normed.astype(BF).reshape(nf, local_len, width)
    late = jnp.concatenate([partial_normed, partial_out[:, cut:], pair], axis=1)
    gram = gram_of(lax.optimization_barrier((s_pieces, late))[0])
    gram_other = xor_swap(gram, 1, nr)
    late = z_exchange(after(late, grad_got))

    ortho = orthogonalize(out_plane, gram, gram_other, s_cols, nf)
    back = z_exchange(after(ortho, late))
    late = after(late, back)
    ortho_mine = jnp.stack([jnp.where(is_out, back[1], back[0]), back[2], back[3]])
    ortho_pieces = with_partner(plane_pieces(ortho_mine, 1, nr), nr)

    mats = (qkv_weight, out_weight, up_weight, down_weight)
    moments = (qkv_moment, out_moment, up_moment, down_moment)
    grad_pieces = with_partner(grad_pieces, nr)
    grad_rules = [grad_rule] * 4
    done = finish(grad_pieces, moments, grad_rules, 2, nr, (0, 1, 2, 3))
    grads, new_moments = [d[0] for d in done], [d[1] for d in done]
    rules = [weight_rule(MATRIX_RATE * 0.2 * math.sqrt(w.shape[1])) for w in mats]
    new_mats = [d[0] for d in finish(ortho_pieces, mats, rules, 1, nr, (0, 1, 2, 3))]

    inputs = tok.astype(F32)
    rest = local_len - cut
    summed = jnp.concatenate([jnp.sum(x.astype(F32), axis=0) for x in (summed, late[:, local_len : local_len + rest])])
    block_out = (inputs + summed + down_bias_full).astype(BF)
    d_normed = jnp.sum(late[:, :local_len].astype(F32), axis=0)
    xhat, inv_std = layer_norm_parts(inputs)
    e = d_normed * gain
    input_grad = cot.astype(F32) + inv_std * (
        e - jnp.mean(e, axis=-1, keepdims=True) - xhat * jnp.mean(e * xhat, axis=-1, keepdims=True)
    )

    pair = jnp.sum(late[:, local_len + rest : local_len + rest + 2, :rows].astype(F32), axis=0).reshape(2 * rows)
    down_sum = jnp.sum(lax.dynamic_slice_in_dim(cot_all, f * rows, rows, 1).astype(F32), axis=0)
    up_sum = up_sum.reshape(hidden_width)
    small = plane_sum_small(jnp.concatenate([pair, down_sum, up_sum]), nr)
    vec_grads = [small[:rows], small[rows : 2 * rows], small[3 * rows :], small[2 * rows : 3 * rows]]
    vec_moments = [
        MOMENTUM_RATE * m + g
        for m, g in zip((gain_moment, beta_moment, up_bias_moment, down_bias_moment), vec_grads)
    ]
    vec_new = [
        p.astype(F32) - VECTOR_RATE * m for p, m in zip((ln_gain, ln_bias, up_bias, down_bias), vec_moments)
    ]

    return (
        block_out.reshape(1, local_len, width),
        input_grad.reshape(1, local_len, width),
        *grads,
        *vec_grads,
        *new_mats,
        *vec_new,
        *new_moments,
        *vec_moments,
    )


def solution(mesh):
    split3 = P("rep", "fsdp", None)
    mat = P("fsdp", None)
    vec = P("fsdp")

    return jax.shard_map(
        on_device,
        mesh=mesh,
        in_specs=(split3,) * 2 + (mat,) * 4 + (vec,) * 4 + (mat,) * 4 + (vec,) * 4,
        out_specs=(split3,) * 2 + ((mat,) * 4 + (vec,) * 4) * 3,
        check_vma=False,
    )
```
